32 devices in a mesh: seq: 8 (over z, x), tp: 4 (over y, core).
Axes of the slice: x: 2, y: 2, z: 4, core: 2. Of those that a mesh axis runs over, the one named last changes fastest.
Arguments:
- queries: bfloat16 [4096, 4096], P('seq', 'tp'), may hold values from -6 to 6
- keys: bfloat16 [4096, 4096], P('seq', 'tp'), may hold values from -6 to 6
- values: bfloat16 [4096, 4096], P('seq', 'tp'), may hold values from -6 to 6
- log_decay: float32 [4096, 32], P('seq', 'tp'), may hold values from -1.2 to 0, as said below
- out_weight: bfloat16 [4096, 6144], P('tp', 'seq'), may hold values from -0.09375 to 0.09375
- grad_out: bfloat16 [4096, 6144], P('seq', 'tp'), may hold values from -6 to 6
Outputs:
- grad_queries: bfloat16 [4096, 4096], P('seq', 'tp')
- grad_keys: bfloat16 [4096, 4096], P('seq', 'tp')
- grad_values: bfloat16 [4096, 4096], P('seq', 'tp')
- grad_weight: float32 [6144, 4096], P('seq', 'tp')
The draws below stay inside these ranges and needn't reach their ends.
Inputs may be any that keep to these rules, and one draw needn't show every extreme that they name: `log_decay`: log decay of each head's state at each token.
All inputs are finite; a program needn't handle non-finite values.
Results may differ from the reference program's by a relative error of at most 0.0029.
Values may be sent and summed in bfloat16 or wider, within the bound.
A program may use at most 192 MiB of HBM per device.

```python
import math
import jax
import jax.numpy as jnp
from jax import lax

D = 6144
SHARD_ATTN_UNITS = 32
DH = 128
BLOCK = 256
TOK_DEV = 512
STREAM_LENGTH = 4096
HD = 4096


def draw_log_decay(key, part):
    parts_keys = jax.random.split(jax.random.fold_in(key, 17), 6)
    share = 0.5
    fast = jax.random.uniform(parts_keys[0], (SHARD_ATTN_UNITS,)) < share
    fast_rate = jnp.exp(jax.random.uniform(parts_keys[1], (SHARD_ATTN_UNITS,), minval=math.log(1.0 / 50.0), maxval=math.log(1.0 / 30.0)))
    slow_rate = 0.25 / STREAM_LENGTH
    nominal_speed = jnp.where(fast, fast_rate, slow_rate)
    device_blocks = STREAM_LENGTH // TOK_DEV
    processor_factor = jnp.exp(jax.random.uniform(parts_keys[2], (device_blocks, SHARD_ATTN_UNITS), minval=math.log(0.5), maxval=math.log(2.0)))
    processor_factor = jnp.repeat(processor_factor, TOK_DEV, axis=0)
    rough_estimate = jax.random.uniform(parts_keys[3], (STREAM_LENGTH, SHARD_ATTN_UNITS), minval=0.5, maxval=1.5)
    spot_names = jax.random.randint(parts_keys[4], (3, SHARD_ATTN_UNITS), 0, STREAM_LENGTH)
    objective_scores = jax.random.uniform(parts_keys[5], (3, SHARD_ATTN_UNITS), minval=0.6, maxval=0.8)
    word_indices = jnp.arange(STREAM_LENGTH)[:, None]
    spike_occurrences = jnp.zeros((STREAM_LENGTH, SHARD_ATTN_UNITS), jnp.float32)
    for picking_mask in range(3):
        spike_occurrences = spike_occurrences + jnp.where(word_indices == spot_names[picking_mask][None, :], jnp.log(objective_scores[picking_mask])[None, :], 0.0)
    return (spike_occurrences - nominal_speed[None, :] * processor_factor * rough_estimate).astype(jnp.float32)


def raised(array, stream_key, source, target, parts, factor):
    def block_of(dim):
        return (jnp.arange(array.shape[dim]) // (array.shape[dim] // parts)).reshape((-1,) + (1,) * (array.ndim - 1 - dim))

    near = jax.random.permutation(stream_key, parts)[block_of(target)]
    far = (block_of(target) + parts // 2) % parts
    return jnp.where((block_of(source) == near) | (block_of(source) == far), factor * array, array)


def block_scale(stream_key, dims, shards, smallest, high):
    loudness = 1.0
    for dim, parts in shards:
        steps = jax.random.uniform(jax.random.fold_in(jax.random.fold_in(stream_key, 6), dim), (parts,), jnp.float32, smallest / len(shards), high / len(shards))
        loudness = loudness * jnp.repeat(jnp.exp(steps), dims[dim] // parts).reshape((-1,) + (1,) * (len(dims) - 1 - dim))
    return loudness


def noise(own_key, dims, spread, limit, shards=(), held_as=jnp.bfloat16):
    values = spread * jax.random.normal(own_key, dims, jnp.float32)
    if shards:
        values = values * block_scale(own_key, dims, shards, -0.22, 0.18)
    return jnp.clip(values, -limit, limit).astype(held_as)


def noise_with(rng, shape, width, reach, pieces, heavy, dtype=jnp.bfloat16):
    values = width * jax.random.normal(rng, shape, jnp.float32)
    if pieces:
        values = values * block_scale(rng, shape, pieces, -0.22, 0.18)
    return jnp.clip(raised(values, jax.random.fold_in(rng, 3), *heavy), -reach, reach).astype(dtype)


def setup_inputs(seed: int = 0) -> dict:
    seeds = jax.random.split(jax.random.key(seed), 7)
    queries = noise(seeds[0], (STREAM_LENGTH, HD), 1.0, 6.0, ((0, 8), (1, 4)))
    keys = noise(seeds[1], (STREAM_LENGTH, HD), 1.0, 6.0, ((0, 8), (1, 4)))
    values = noise(seeds[2], (STREAM_LENGTH, HD), 1.0, 6.0, ((0, 8), (1, 4)))
    log_decay = draw_log_decay(jax.random.fold_in(seeds[6], 71), 0)
    out_weight = noise(seeds[4], (HD, D), HD ** -0.5, 0.09375, ((0, 4), (1, 8)))
    grad_out = noise_with(seeds[5], (STREAM_LENGTH, D), 1.0, 6.0, ((0, 8), (1, 4)), (0, 1, 8, 2.0))
    return dict(queries=queries, keys=keys, values=values, log_decay=log_decay, out_weight=out_weight, grad_out=grad_out)


EPS = 1e-06
HIGH = lax.Precision.HIGHEST

def attend(query_f, key_f, value_f, rates):
    blocks = query_f.shape[0] // BLOCK
    shape4 = (blocks, BLOCK, SHARD_ATTN_UNITS, DH)
    lower = jnp.arange(BLOCK)[:, None] >= jnp.arange(BLOCK)[None, :]

    def advance(state, item):
        query_b, key_b, value_b, rate_b = item
        cumul = jnp.cumsum(rate_b, axis=0)
        cumul_t = cumul.T
        decay_mat = jnp.where(lower[None], jnp.exp(jnp.minimum(cumul_t[:, :, None] - cumul_t[:, None, :], 0.0)), 0.0)
        scores = jnp.einsum('thd,shd->hts', query_b, key_b, precision=HIGH) * decay_mat
        inner = jnp.einsum('hts,shd->thd', scores, value_b, precision=HIGH)
        outer = jnp.exp(cumul)[:, :, None] * jnp.einsum('thd,hde->the', query_b, state, precision=HIGH)
        total = cumul[-1]
        into_end = jnp.exp(total[None, :] - cumul)
        fresh = jnp.exp(total)[:, None, None] * state + jnp.einsum('th,thd,the->hde', into_end, key_b, value_b, precision=HIGH)
        return (fresh, inner + outer)
    start = jnp.zeros((SHARD_ATTN_UNITS, DH, DH), jnp.float32)
    items = (query_f.reshape(shape4), key_f.reshape(shape4), value_f.reshape(shape4), rates.reshape(blocks, BLOCK, SHARD_ATTN_UNITS))
    final, outputs = lax.scan(jax.checkpoint(advance), start, items)
    return outputs.reshape(STREAM_LENGTH, SHARD_ATTN_UNITS, DH)

def reference(queries, keys, values, log_decay, out_weight, grad_out):
    query_f = queries.astype(jnp.float32).reshape(STREAM_LENGTH, SHARD_ATTN_UNITS, DH)
    key_f = keys.astype(jnp.float32).reshape(STREAM_LENGTH, SHARD_ATTN_UNITS, DH)
    value_f = values.astype(jnp.float32).reshape(STREAM_LENGTH, SHARD_ATTN_UNITS, DH)

    def forward(query_a, key_a, value_a):
        attended = attend(query_a, key_a, value_a, log_decay)
        scale = jnp.sqrt(lax.optimization_barrier(jnp.mean(attended * attended, axis=-1, keepdims=True)) + EPS)
        return attended / scale
    o_hat, pullback = jax.vjp(forward, query_f, key_f, value_f)
    normed = o_hat.reshape(STREAM_LENGTH, HD).astype(jnp.bfloat16)
    grad_normed = jnp.dot(grad_out, out_weight.T, preferred_element_type=jnp.float32)
    grad_q, grad_k, grad_v = pullback(grad_normed.reshape(STREAM_LENGTH, SHARD_ATTN_UNITS, DH))
    grad_weight = jnp.dot(grad_out.T, normed, preferred_element_type=jnp.float32)
    return (grad_q.reshape(STREAM_LENGTH, HD).astype(jnp.bfloat16), grad_k.reshape(STREAM_LENGTH, HD).astype(jnp.bfloat16), grad_v.reshape(STREAM_LENGTH, HD).astype(jnp.bfloat16), grad_weight)
```

```python
import jax
import jax.numpy as jnp
from jax import lax
from jax.experimental import pallas as pl
from jax.experimental.pallas import tpu as pltpu
from jax.sharding import PartitionSpec as P

SUB = 256
EPS = 1e-06
F32 = jnp.float32
BF16 = jnp.bfloat16


def halves(x):
    high = x.astype(BF16)
    return high, (x - high.astype(F32)).astype(BF16)


def dot(a, b, ca, cb):
    return lax.dot_general(a, b, (((ca,), (cb,)), ((), ())), preferred_element_type=F32)


def wide_left(a, b, ca, cb):
    high, low = halves(a)
    return dot(high, b, ca, cb) + dot(low, b, ca, cb)


def wide_right(a, b, ca, cb):
    high, low = halves(b)
    return dot(a, high, ca, cb) + dot(a, low, ca, cb)


def wide_both(a, b, ca, cb):
    ah, al = halves(a)
    bh, bl = halves(b)
    return dot(ah, bh, ca, cb) + (dot(ah, bl, ca, cb) + dot(al, bh, ca, cb))


def decay_between(col, row, diagonal):
    weight = jnp.exp(jnp.minimum(col - row, 0.0))
    if diagonal:
        shape = weight.shape
        lower = lax.broadcasted_iota(jnp.int32, shape, 0) >= lax.broadcasted_iota(jnp.int32, shape, 1)
        weight = jnp.where(lower, weight, 0.0)
    return weight


def state_kernel(k_ref, v_ref, col_ref, state_ref):
    col = col_ref[0]
    total = col[-1:, :]
    state_ref[0] = wide_right(k_ref[...], jnp.exp(total - col) * v_ref[...].astype(F32), 0, 0)


def forward_kernel(q_ref, k_ref, v_ref, col_ref, row_ref, state_ref, att_ref, normed_ref):
    rows = q_ref.shape[0]
    state = state_ref[0]
    for t in range(0, rows, SUB):
        query = q_ref[t : t + SUB, :]
        col = col_ref[0, t : t + SUB, :]
        total = jnp.exp(col) * wide_right(query, state, 1, 0)
        for s in range(0, t + 1, SUB):
            weight = decay_between(col, row_ref[0, :, s : s + SUB], s == t)
            scores = dot(query, k_ref[s : s + SUB, :], 1, 1) * weight
            total = total + wide_left(scores, v_ref[s : s + SUB, :], 1, 0)
        att_ref[t : t + SUB, :] = total
        scale = jnp.sqrt(jnp.mean(total * total, axis=-1, keepdims=True) + EPS)
        normed_ref[t : t + SUB, :] = (total / scale).astype(BF16)


def cotangent_kernel(q_ref, col_ref, att_ref, gn_ref, ga_ref, grad_ref):
    att = att_ref[...]
    scale = jnp.sqrt(jnp.mean(att * att, axis=-1, keepdims=True) + EPS)
    o_hat = att / scale
    gn = gn_ref[...]
    ga = (gn - o_hat * jnp.mean(gn * o_hat, axis=-1, keepdims=True)) / scale
    ga_ref[...] = ga
    grad_ref[0] = wide_right(q_ref[...], jnp.exp(col_ref[0]) * ga, 0, 0)


def backward_kernel(
    q_ref, k_ref, v_ref, ga_ref, col_ref, row_ref, state_ref, end_ref, gq_ref, gk_ref, gv_ref
):
    rows = q_ref.shape[0]
    state = state_ref[0]
    end = end_ref[0]
    col_all = col_ref[0]
    into_end = jnp.exp(col_all[-1:, :] - col_all)
    starts = range(0, rows, SUB)
    gk = {}
    gv = {}
    for s in starts:
        tail = into_end[s : s + SUB, :]
        gk[s] = tail * wide_right(v_ref[s : s + SUB, :], end, 1, 1)
        gv[s] = tail * wide_right(k_ref[s : s + SUB, :], end, 1, 0)
    for t in starts:
        query = q_ref[t : t + SUB, :]
        ga = ga_ref[t : t + SUB, :]
        col = col_all[t : t + SUB, :]
        gq = jnp.exp(col) * wide_both(ga, state, 1, 1)
        for s in range(0, t + 1, SUB):
            key = k_ref[s : s + SUB, :]
            weight = decay_between(col, row_ref[0, :, s : s + SUB], s == t)
            scores = dot(query, key, 1, 1) * weight
            mix = wide_left(ga, v_ref[s : s + SUB, :], 1, 1) * weight
            gq = gq + wide_left(mix, key, 1, 0)
            gk[s] = gk[s] + wide_left(mix, query, 0, 0)
            gv[s] = gv[s] + wide_both(scores, ga, 0, 0)
        gq_ref[t : t + SUB, :] = gq.astype(BF16)
    for s in starts:
        gk_ref[s : s + SUB, :] = gk[s].astype(BF16)
        gv_ref[s : s + SUB, :] = gv[s].astype(BF16)


def per_head(kernel, heads, rows, size, ins, outs, flops):
    kinds = {
        "tok": pl.BlockSpec((rows, size), lambda h: (0, h)),
        "col": pl.BlockSpec((1, rows, 1), lambda h: (h, 0, 0)),
        "row": pl.BlockSpec((1, 1, rows), lambda h: (h, 0, 0)),
        "state": pl.BlockSpec((1, size, size), lambda h: (h, 0, 0)),
    }
    shapes = {"tok": (rows, heads * size), "state": (heads, size, size)}
    return pl.pallas_call(
        kernel,
        grid=(heads,),
        in_specs=[kinds[kind] for kind in ins],
        out_specs=[kinds[kind] for kind, _ in outs],
        out_shape=[jax.ShapeDtypeStruct(shapes[kind], dtype) for kind, dtype in outs],
        compiler_params=pltpu.CompilerParams(vmem_limit_bytes=32 * 2**20),
        cost_estimate=pl.CostEstimate(
            flops=flops, bytes_accessed=4 * rows * heads * size * 2, transcendentals=0
        ),
    )


def seq_permute(x, send):
    count = lax.axis_size("seq")
    pairs = [(i, send(i)) for i in range(count)]
    return lax.ppermute(x, "seq", [(i, to) for i, to in pairs if 0 <= to < count])


def tp_blocks(x):
    count, mine = lax.axis_size("tp"), lax.axis_index("tp")
    blocks = []
    for hop in range(count // 2):
        block = x
        if hop:
            block = lax.ppermute(x, "tp", [(i, (i + 2 * hop) % count) for i in range(count)])
        place = lax.rem(mine + count - 2 * hop, count)
        blocks.append((place, block))
        other = place + 1 - 2 * lax.rem(place, 2)
        blocks.append((other, lax.ppermute(block, "tp", [(i, i ^ 1) for i in range(count)])))
    return blocks


def carried_in(log, state, backward):
    heads, size, _ = state.shape
    count, mine = lax.axis_size("seq"), lax.axis_index("seq")
    side = lax.rem(mine, 2)
    near = (side == 0) if backward else (side == 1)

    def packed(log, state):
        return jnp.concatenate(
            [state, jnp.broadcast_to(log[:, None, None], (heads, 8, size))], axis=1
        )

    def split(pack):
        return pack[:, size, 0], pack[:, :size, :]

    def decayed(log, state):
        return jnp.exp(log)[:, None, None] * state

    pair_log, pair_state = split(seq_permute(packed(log, state), lambda i: i ^ 1))
    both = jnp.where(near, decayed(log, pair_state) + state, decayed(pair_log, state) + pair_state)
    mine_pack = packed(log + pair_log, both)
    total = jnp.zeros_like(state)
    passed = jnp.zeros_like(log)
    for hop in range(1, count // 2):
        step = -2 * hop if backward else 2 * hop
        far_log, far_state = split(seq_permute(mine_pack, lambda i: i + step))
        total = total + decayed(passed, far_state)
        passed = passed + far_log
    return jnp.where(near, decayed(pair_log, total) + pair_state, total)


def prefix(log_decay):
    rows = log_decay.shape[0]
    upto = jnp.tril(jnp.ones((rows, rows), F32))
    return lax.dot_general(
        log_decay, upto, (((0,), (1,)), ((), ())), precision=lax.Precision.HIGHEST, preferred_element_type=F32
    )


def on_device_any(queries, keys, values, log_decay, out_weight, grad_out):
    rows, heads = log_decay.shape
    size = queries.shape[1] // heads
    count, mine = lax.axis_size("seq"), lax.axis_index("seq")
    tps = lax.axis_size("tp")

    weight_all = lax.all_gather(out_weight, "seq", axis=1, tiled=True)
    cotangent = tp_blocks(grad_out)

    cumul = prefix(log_decay)
    row = cumul[:, None, :]
    col = cumul[:, :, None]
    dev_log = cumul[:, -1]
    unit = 2 * rows * heads * size * size
    (dev_state,) = per_head(
        state_kernel, heads, rows, size, ("tok", "tok", "col"), (("state", F32),), 2 * unit
    )(keys, values, col)
    state_in = carried_in(dev_log, dev_state, False)

    grad_out, state_in = lax.optimization_barrier((grad_out, state_in))
    share = count // tps
    width = grad_out.shape[1] // share
    arrived = jnp.zeros((share, rows, width), grad_out.dtype)
    for turn in range(share):
        pairs = []
        for i in range(count):
            for j in range(tps):
                to = (share * j + (i % share + turn) % share) * tps + i // share
                pairs.append((i * tps + j, to))
        block = lax.rem(lax.rem(mine, share) + turn, share)
        piece = lax.dynamic_slice_in_dim(grad_out, block * width, width, axis=1)
        piece = lax.ppermute(piece, ("seq", "tp"), pairs)
        slot = lax.rem(lax.rem(mine, share) + share - turn, share)
        arrived = lax.dynamic_update_slice_in_dim(arrived, piece[None], slot, axis=0)
    by_columns = tp_blocks(arrived.reshape(share * rows, width))

    attended, normed = per_head(
        forward_kernel,
        heads,
        rows,
        size,
        ("tok", "tok", "tok", "col", "row", "state"),
        (("tok", F32), ("tok", BF16)),
        12 * unit,
    )(queries, keys, values, col, row, state_in)
    own_cot, own_columns = [cotangent[0][1]], [by_columns[0][1]]
    normed, weight_all, late_cot, late_columns = lax.optimization_barrier(
        (
            normed,
            weight_all,
            [block for _, block in cotangent[1:]],
            [block for _, block in by_columns[1:]],
        )
    )
    cotangent = [(at, x) for (at, _), x in zip(cotangent, own_cot + late_cot)]
    by_columns = [(at, x) for (at, _), x in zip(by_columns, own_columns + late_columns)]
    normed_all = lax.all_gather(normed, "seq", axis=0, tiled=True)

    grad_normed = jnp.zeros((rows, heads * size), F32)
    for place, block in cotangent:
        part = lax.dynamic_slice_in_dim(weight_all, place * share * width, share * width, axis=1)
        grad_normed = grad_normed + lax.dot_general(
            block, part, (((1,), (1,)), ((), ())), preferred_element_type=F32
        )
    grad_att, dev_grad = per_head(
        cotangent_kernel,
        heads,
        rows,
        size,
        ("tok", "col", "tok", "tok"),
        (("tok", F32), ("state", F32)),
        2 * unit,
    )(queries, col, attended, grad_normed)
    end_grad = carried_in(dev_log, dev_grad, True)
    grad_q, grad_k, grad_v = per_head(
        backward_kernel,
        heads,
        rows,
        size,
        ("tok", "tok", "tok", "tok", "col", "row", "state", "state"),
        (("tok", BF16), ("tok", BF16), ("tok", BF16)),
        40 * unit,
    )(queries, keys, values, grad_att, col, row, state_in, end_grad)
    grad_weight = jnp.zeros((width, heads * size), F32)
    for place, block in by_columns:
        part = lax.dynamic_slice_in_dim(normed_all, place * share * rows, share * rows, axis=0)
        grad_weight = grad_weight + lax.dot_general(
            block, part, (((0,), (0,)), ((), ())), preferred_element_type=F32
        )
    return grad_q, grad_k, grad_v, grad_weight


MESH = pl.DeviceIdType.MESH
ZS = 4
TPS = 4
CHUNKS = 4


def fused_kernel(
    q_in, k_in, v_in, w_in, g_in, col_ref, row_ref,
    gq_out, gk_out, gv_out, dw_out,
    q_ref, k_ref, v_ref, g1, g2, relay, wb, nb, att, gn, xs, xr, go,
    sl, px, zin, zout, si, gl, bx, bin_, bout, ds, dr, dw,
    loc, g_recv, gs1, gs2, gs3, w_recv, w_send, rb_send, rb_recv, g2_recv, g2s1, g2s2, g2s3,
    n_recv, n_send, x_send, x_recv, go_send, gn_recv, sx_send, sx_recv, zc_send, zc_recv,
    bx_send, bx_recv, bz_send, bz_recv, d_send, d_recv,
):
    rows, columns = q_ref.shape
    heads, _, size = si.shape
    width = w_in.shape[1]
    per = heads // CHUNKS
    wide = per * size
    seq, tp = lax.axis_index("seq"), lax.axis_index("tp")
    z, x = lax.div(seq, 2), lax.rem(seq, 2)
    y, core = lax.div(tp, 2), lax.rem(tp, 2)
    inside = lax.rem(lax.div(z + 1, 2), 2)
    inner, outer = inside == 1, inside == 0
    i_z = 1 + lax.div(z, 2)
    o_z = 3 * lax.div(z, 2)
    mid, far = 3 - i_z, 3 - o_z
    part = i_z + o_z - z
    other_x = 1 - x
    tp_y, tp_s, tp_d = (1 - y) * 2 + core, y * 2 + 1 - core, (1 - y) * 2 + 1 - core

    def at(zz, xx, tt):
        return (zz * 2 + xx, tt)

    here_x = at(z, other_x, tp)
    here_y = at(z, x, tp_y)
    here_s = at(z, x, tp_s)

    def copy(src, dst, send, recv, to):
        return pltpu.make_async_remote_copy(
            src_ref=src, dst_ref=dst, send_sem=send, recv_sem=recv, device_id=to, device_id_type=MESH
        )

    ends = []

    def go_copy(c, when=None):
        ends.append((c, when))
        if when is None:
            c.start()
        else:
            pl.when(when)(c.start)

    barrier = pltpu.get_barrier_semaphore()
    peers = [at(lax.rem(z + d, ZS), x, tp) for d in range(1, ZS)]
    peers += [here_x, at(part, other_x, tp), here_y, here_s]
    for peer in peers:
        pl.semaphore_signal(barrier, inc=1, device_id=peer, device_id_type=MESH)
    pl.semaphore_wait(barrier, len(peers))

    loads = [
        pltpu.make_async_copy(a, b, loc.at[n])
        for n, (a, b) in enumerate(((q_in, q_ref), (k_in, k_ref), (v_in, v_ref)))
    ]
    own_g = pltpu.make_async_copy(
        g_in.at[:, pl.ds(pl.multiple_of(x * width, width), width)], g1.at[0, tp], loc.at[3]
    )
    own_w = pltpu.make_async_copy(w_in, wb.at[z], loc.at[4])

    def half(n):
        return g_in.at[:, pl.ds(pl.multiple_of(n * width, width), width)]

    go_copy(
        copy(half(other_x), g1.at[1 + 2 * (1 - inside), tp], gs1.at[0],
             g_recv.at[1 + 2 * (1 - inside), tp], at(i_z, other_x, tp))
    )

    def w_chunk(n):
        part_rows = pl.ds(n * wide, wide)
        go_copy(copy(w_in.at[part_rows], wb.at[z, part_rows], w_send.at[0, n], w_recv.at[z, n], at(mid, x, tp)))
        go_copy(
            copy(w_in.at[part_rows], wb.at[z, part_rows], w_send.at[1, n], w_recv.at[z, n], at(i_z, x, tp)),
            outer,
        )

    @pl.when(inner)
    def _():
        own_g.start()
        own_w.start()

    for c in loads:
        c.start()
    w_chunk(0)

    def spread(s, wait=None):
        if wait is not None:
            pl.when(inner)(wait)
        for n, to in enumerate((here_y, here_s)):
            go_copy(copy(g1.at[s, tp], g1.at[s, tp], gs2.at[s, n], g_recv.at[s, tp], to), inner)

    def g_got(s, t):
        return copy(g1.at[s, t], g1.at[s, t], gs3.at[s], g_recv.at[s, t], here_s)

    def pass_on(s):
        pl.when(inner)(g_got(s, tp_y).wait_recv)
        go_copy(g_got(s, tp_y), inner)

    spread(0, own_g.wait)
    go_copy(copy(half(1), relay, rb_send, rb_recv, here_y))
    for c in loads:
        c.wait()

    def columns_of(h):
        return pl.ds(pl.multiple_of(h * size, size), size)

    def local_state(h, _):
        col = col_ref[h]
        total = col[-1:, :]
        at_h = columns_of(h)
        sl[h, 0:size, :] = wide_right(k_ref[:, at_h], jnp.exp(total - col) * v_ref[:, at_h].astype(F32), 0, 0)
        sl[h, size:, :] = jnp.broadcast_to(total, (8, size))
        return 0

    lax.fori_loop(0, heads, local_state, 0)
    sx = copy(sl, px, sx_send, sx_recv, here_x)
    go_copy(sx)

    spread(1, g_got(1, tp).wait_recv)
    pass_on(0)
    sx.wait_recv()

    def chain(n, have, forward):
        mine, pair, came, leaves, result = (sl, px, zin, zout, si) if forward else (gl, bx, bin_, bout, gl)

        def one(j, _):
            h = n * per + j
            log_own, log_pair = sl[h, size : size + 1, :], px[h, size : size + 1, :]
            own, other = mine[h, 0:size, :], pair[h, 0:size, :]
            near = (x == 1) if forward else (x == 0)
            both = jnp.where(near, jnp.exp(log_own) * other + own, jnp.exp(log_pair) * own + other)
            if have:
                total = came[h]
                leaves[h] = jnp.exp(log_own + log_pair) * total + both
                result[h] = jnp.where(near, jnp.exp(log_pair) * total + other, total)
            else:
                leaves[h] = both
                result[h] = jnp.where(near, other, jnp.zeros_like(other))
            return 0

        lax.fori_loop(0, per, one, 0)

    def z_send(n):
        part_heads = pl.ds(n * per, per)
        return copy(zout.at[part_heads], zin.at[part_heads], zc_send.at[n], zc_recv.at[n], at(lax.rem(z + 1, ZS), x, tp))

    def b_send(n):
        part_heads = pl.ds(n * per, per)
        return copy(bout.at[part_heads], bin_.at[part_heads], bz_send.at[n], bz_recv.at[n], at(lax.rem(z + 3, ZS), x, tp))

    def chunks(body, start=0, stop=CHUNKS):
        def step(n, _):
            body(n)
            return 0

        lax.fori_loop(start, stop, step, 0)

    @pl.when(z == 0)
    def _():
        @chunks
        def _(n):
            chain(n, False, True)
            z_send(n).start()

    go_copy(copy(half(x), g1.at[2, tp], gs1.at[1], g_recv.at[2, tp], at(i_z, x, tp)), outer)
    w_chunk(1)
    pass_on(1)
    spread(3, g_got(3, tp).wait_recv)

    @pl.when(z > 0)
    def _():
        @chunks
        def _(n):
            z_send(n).wait_recv()
            chain(n, True, True)
            pl.when(z < ZS - 1)(z_send(n).start)

    w_chunk(2)
    w_chunk(3)
    z_a, z_b = tp, tp_y
    a_here = pltpu.make_async_copy(half(0), g2.at[0, z], loc.at[5])
    b_here = pltpu.make_async_copy(relay, g2.at[1, z], loc.at[6])
    copy(relay, relay, rb_send, rb_recv, here_y).wait_recv()
    pl.when(z_a == z)(a_here.start)
    pl.when(z_b == z)(b_here.start)
    go_copy(copy(half(0), g2.at[0, z], g2s1.at[0], g2_recv.at[0, z], at(z_a, x, tp)), z_a != z)
    go_copy(copy(relay, g2.at[1, z], g2s1.at[1], g2_recv.at[1, z], at(z_b, x, tp)), z_b != z)

    def n_copy(n, src, way, to):
        return copy(nb.at[src, n], nb.at[src, n], n_send.at[way, n], n_recv.at[src, n], at(to, x, tp))

    @chunks
    def _(n):
        def one(j, _):
            h = n * per + j
            at_h = columns_of(h)
            state = si[h]
            for t in range(0, rows, SUB):
                query = q_ref[t : t + SUB, at_h]
                col = col_ref[h, t : t + SUB, :]
                total = jnp.exp(col) * wide_right(query, state, 1, 0)
                for s in range(0, t + 1, SUB):
                    weight = decay_between(col, row_ref[h, :, s : s + SUB], s == t)
                    scores = dot(query, k_ref[s : s + SUB, at_h], 1, 1) * weight
                    total = total + wide_left(scores, v_ref[s : s + SUB, at_h], 1, 0)
                att[t : t + SUB, at_h] = total
                scale = jnp.sqrt(jnp.mean(total * total, axis=-1, keepdims=True) + EPS)
                nb[z, n, t : t + SUB, columns_of(j)] = (total / scale).astype(BF16)
            return 0

        lax.fori_loop(0, per, one, 0)
        n_copy(n, z, 0, part).start()
        pl.when(inner)(n_copy(n, z, 1, mid).start)

    spread(2, g_got(2, tp).wait_recv)
    pass_on(3)

    def w_got(src, n):
        part_rows = pl.ds(n * wide, wide)
        return copy(wb.at[src, part_rows], wb.at[src, part_rows], w_send.at[0, n], w_recv.at[src, n], at(mid, x, tp))

    def product(s, n, r):
        total = None
        for t in range(TPS):
            one = dot(g1[s, t, pl.ds(r * SUB, SUB), :], wb[t, pl.ds(n * wide, wide), :], 1, 1)
            total = one if total is None else total + one
        return total

    def x_copy(n, k):
        return copy(xs.at[n, k], xr.at[n, k], x_send.at[n, k], x_recv.at[n, k], here_x)

    def row_blocks(body):
        def step(r, _):
            body(r)
            return 0

        lax.fori_loop(0, rows // SUB, step, 0)

    @pl.when(inner)
    def _():
        own_w.wait()
        for s in (1, 3):
            for t in (tp_s, tp_d):
                g_got(s, t).wait_recv()

        @chunks
        def _(n):
            for d in range(1, ZS):
                w_got(lax.rem(z + d, ZS), n).wait_recv()
            for k, s in enumerate((1, 3)):

                @row_blocks
                def _(r, k=k, s=s):
                    xs[n, k, pl.ds(r * SUB, SUB), :] = product(s, n, r).astype(BF16)

                x_copy(n, k).start()

    pass_on(2)

    primary = core == lax.rem(z, 2)
    own_half = lax.rem(lax.div(z, 2) + y, 2)

    def g2_copy(hf, src, send, to):
        return copy(g2.at[hf, src], g2.at[hf, src], send, g2_recv.at[hf, src], to)

    for d in range(ZS):
        src = lax.rem(z + d, ZS)

        @pl.when(primary)
        def _(d=d, src=src):
            if d == 0:
                pl.when(z_a == z)(a_here.wait)
                pl.when(z_b == z)(b_here.wait)
            else:
                g2_copy(own_half, src, g2s2.at[d, 0], here_y).wait_recv()

        for n, to in enumerate((here_y, here_s)):
            go_copy(g2_copy(own_half, src, g2s2.at[d, n], to), primary)

    @pl.when(inner)
    def _():
        for s in (0, 2):
            for t in (tp_s, tp_d):
                g_got(s, t).wait_recv()

        @chunks
        def _(n):
            for k, s in enumerate((0, 2)):
                x_copy(n, k).wait_recv()

                @row_blocks
                def _(r, k=k, s=s):
                    at_r = pl.ds(r * SUB, SUB)
                    total = product(s, n, r) + xr[n, k, at_r, :].astype(F32)
                    if k == 0:
                        gn[n, at_r, :] = total
                    else:
                        go[n, at_r, :] = total

            copy(go.at[n], gn.at[n], go_send.at[n], gn_recv.at[n], at(part, x, tp)).start()
            n_copy(n, part, 2, mid).wait_recv()
            n_copy(n, part, 2, mid).start()
            n_copy(n, mid, 3, part).wait_recv()
            n_copy(n, mid, 3, part).start()

    for d in range(ZS):
        src = lax.rem(z + d, ZS)

        @pl.when(primary)
        def _(d=d, src=src):
            g2_copy(1 - own_half, src, g2s3.at[d], here_s).wait_recv()

        go_copy(g2_copy(1 - own_half, src, g2s3.at[d], here_s), primary)

    def bx_copy(n):
        part_heads = pl.ds(n * per, per)
        return copy(gl.at[part_heads], bx.at[part_heads], bx_send.at[n], bx_recv.at[n], here_x)

    @chunks
    def _(n):
        @pl.when(outer)
        def _():
            copy(go.at[n], gn.at[n], go_send.at[n], gn_recv.at[n], at(part, x, tp)).wait_recv()

        @pl.when(inner)
        def _():
            n_copy(n, far, 4, part).wait_recv()
            n_copy(n, far, 4, part).start()

        def one(j, _):
            h = n * per + j
            at_h, at_j = columns_of(h), columns_of(j)
            a = att[:, at_h]
            scale = jnp.sqrt(jnp.mean(a * a, axis=-1, keepdims=True) + EPS)
            o_hat = a / scale
            g = gn[n, :, at_j]
            ga = (g - o_hat * jnp.mean(g * o_hat, axis=-1, keepdims=True)) / scale
            gn[n, :, at_j] = ga
            gl[h] = wide_right(q_ref[:, at_h], jnp.exp(col_ref[h]) * ga, 0, 0)
            return 0

        lax.fori_loop(0, per, one, 0)
        bx_copy(n).start()

    @chunks
    def _(n):
        bx_copy(n).wait()

        @pl.when(z == ZS - 1)
        def _():
            chain(n, False, False)

        @pl.when(z < ZS - 1)
        def _():
            b_send(n).wait_recv()
            chain(n, True, False)

        pl.when(z > 0)(b_send(n).start)

    def backward(n):
        def one(j, _):
            h = n * per + j
            at_h, at_j = columns_of(h), columns_of(j)
            state, end = si[h], gl[h]
            col_all = col_ref[h]
            into_end = jnp.exp(col_all[-1:, :] - col_all)
            starts = range(0, rows, SUB)
            gk, gv, gq = {}, {}, {}
            for s in starts:
                tail = into_end[s : s + SUB, :]
                gk[s] = tail * wide_right(v_ref[s : s + SUB, at_h], end, 1, 1)
                gv[s] = tail * wide_right(k_ref[s : s + SUB, at_h], end, 1, 0)
            for t in starts:
                query = q_ref[t : t + SUB, at_h]
                ga = gn[n, t : t + SUB, at_j]
                col = col_all[t : t + SUB, :]
                gq[t] = jnp.exp(col) * wide_both(ga, state, 1, 1)
                for s in range(0, t + 1, SUB):
                    key = k_ref[s : s + SUB, at_h]
                    weight = decay_between(col, row_ref[h, :, s : s + SUB], s == t)
                    scores = dot(query, key, 1, 1) * weight
                    mix = wide_left(ga, v_ref[s : s + SUB, at_h], 1, 1) * weight
                    gq[t] = gq[t] + wide_left(mix, key, 1, 0)
                    gk[s] = gk[s] + wide_left(mix, query, 0, 0)
                    gv[s] = gv[s] + wide_both(scores, ga, 0, 0)
            for s in starts:
                q_ref[s : s + SUB, at_h] = gq[s].astype(BF16)
                k_ref[s : s + SUB, at_h] = gk[s].astype(BF16)
                v_ref[s : s + SUB, at_h] = gv[s].astype(BF16)
            return 0

        lax.fori_loop(0, per, one, 0)

    def weight_product(hf, n, m):
        total = None
        for src in range(ZS):
            one = dot(g2[hf, src, :, pl.ds(pl.multiple_of(m * SUB, SUB), SUB)], nb[src, n], 0, 0)
            total = one if total is None else total + one
        return total

    def d_copy(n):
        return copy(ds.at[n], dr.at[n], d_send.at[n], d_recv.at[n], here_x)

    def weight_near(n):
        d_copy(n).wait_recv()

        def step(m, _):
            at_m = pl.ds(m * SUB, SUB)
            total = weight_product(x, n, m) + dr[n, at_m, :].astype(F32)
            dw[at_m, pl.ds(pl.multiple_of(n * wide, wide), wide)] = total
            return 0

        lax.fori_loop(0, width // SUB, step, 0)

    @chunks
    def _(n):
        backward(n)

    @pl.when(core != lax.rem(z, 2))
    def _():
        for hf in range(2):
            for src in range(ZS):
                g2_copy(hf, src, g2s3.at[0], here_s).wait_recv()

    def weight_far(n):
        @pl.when(outer)
        def _():
            for d in range(1, ZS):
                n_copy(n, lax.rem(z + d, ZS), 0, part).wait_recv()

        def step(m, _):
            ds[n, pl.ds(m * SUB, SUB), :] = weight_product(other_x, n, m).astype(BF16)
            return 0

        lax.fori_loop(0, width // SUB, step, 0)
        d_copy(n).start()

    chunks(weight_far)
    chunks(weight_near)

    stores = [
        pltpu.make_async_copy(a, b, loc.at[n])
        for n, (a, b) in enumerate(((q_ref, gq_out), (k_ref, gk_out), (v_ref, gv_out), (dw, dw_out)))
    ]
    for c in stores:
        c.start()

    for c, when in ends:
        if when is None:
            c.wait_send()
        else:
            pl.when(when)(c.wait_send)

    @chunks
    def _(n):
        pl.when(z < ZS - 1)(z_send(n).wait_send)
        pl.when(z > 0)(b_send(n).wait_send)
        n_copy(n, z, 0, part).wait_send()
        d_copy(n).wait_send()

        @pl.when(inner)
        def _():
            n_copy(n, z, 1, mid).wait_send()
            n_copy(n, part, 2, mid).wait_send()
            n_copy(n, mid, 3, part).wait_send()
            n_copy(n, far, 4, part).wait_send()
            x_copy(n, 0).wait_send()
            x_copy(n, 1).wait_send()
            copy(go.at[n], gn.at[n], go_send.at[n], gn_recv.at[n], at(part, x, tp)).wait_send()

    for c in stores:
        c.wait()


def on_device(queries, keys, values, log_decay, out_weight, grad_out):
    rows, heads = log_decay.shape
    columns = queries.shape[1]
    size = columns // heads
    width = out_weight.shape[1]
    wide = columns // CHUNKS
    cumul = prefix(log_decay)
    dma = pltpu.SemaphoreType.DMA
    state = pltpu.VMEM((heads, size, size), F32)
    packed = pltpu.VMEM((heads, size + 8, size), F32)
    tokens = pltpu.VMEM((rows, columns), BF16)
    scratch = [
        tokens, tokens, tokens,
        pltpu.VMEM((4, TPS, rows, width), BF16),
        pltpu.VMEM((2, ZS, rows, width), BF16),
        pltpu.VMEM((rows, width), BF16),
        pltpu.VMEM((ZS, columns, width), BF16),
        pltpu.VMEM((ZS, CHUNKS, rows, wide), BF16),
        pltpu.VMEM((rows, columns), F32),
        pltpu.VMEM((CHUNKS, rows, wide), F32),
        pltpu.VMEM((CHUNKS, 2, rows, wide), BF16),
        pltpu.VMEM((CHUNKS, 2, rows, wide), BF16),
        pltpu.VMEM((CHUNKS, rows, wide), F32),
        packed, packed, state, state, state, state, state, state, state,
        pltpu.VMEM((CHUNKS, width, wide), BF16),
        pltpu.VMEM((CHUNKS, width, wide), BF16),
        pltpu.VMEM((width, columns), F32),
        dma((7,)), dma((4, TPS)), dma((2,)), dma((4, 2)), dma((4,)),
        dma((ZS, CHUNKS)), dma((2, CHUNKS)), dma, dma, dma((2, ZS)), dma((2,)), dma((ZS, 2)), dma((ZS,)),
        dma((ZS, CHUNKS)), dma((5, CHUNKS)), dma((CHUNKS, 2)), dma((CHUNKS, 2)), dma((CHUNKS,)), dma((CHUNKS,)),
        dma, dma, dma((CHUNKS,)), dma((CHUNKS,)),
        dma((CHUNKS,)), dma((CHUNKS,)), dma((CHUNKS,)), dma((CHUNKS,)), dma((CHUNKS,)), dma((CHUNKS,)),
    ]
    anywhere, vmem = pl.BlockSpec(memory_space=pl.ANY), pl.BlockSpec(memory_space=pltpu.VMEM)
    token = jax.ShapeDtypeStruct((rows, columns), BF16)
    return pl.pallas_call(
        fused_kernel,
        in_specs=[anywhere] * 5 + [vmem, vmem],
        out_specs=[anywhere] * 4,
        out_shape=[token, token, token, jax.ShapeDtypeStruct((width, columns), F32)],
        scratch_shapes=scratch,
        compiler_params=pltpu.CompilerParams(
            collective_id=0, has_side_effects=True, vmem_limit_bytes=60 * 2**20
        ),
    )(queries, keys, values, out_weight, grad_out, cumul[:, :, None], cumul[:, None, :])


def solution(mesh):
    spec = P("seq", "tp")
    known = dict(mesh.shape) == {"seq": 2 * ZS, "tp": TPS}
    return jax.shard_map(
        on_device if known else on_device_any,
        mesh=mesh,
        in_specs=(spec, spec, spec, spec, P("tp", "seq"), spec),
        out_specs=(spec, spec, spec, spec),
        check_vma=False,
    )
```

```python
import functools

import jax
import jax.numpy as jnp
from jax import lax
from jax.experimental import pallas as pl
from jax.experimental.pallas import tpu as pltpu
from jax.sharding import PartitionSpec as P

SUB = 256
EPS = 1e-06
F32 = jnp.float32
BF16 = jnp.bfloat16


def halves(x):
    high = x.astype(BF16)
    return high, (x - high.astype(F32)).astype(BF16)


def dot(a, b, ca, cb):
    return lax.dot_general(a, b, (((ca,), (cb,)), ((), ())), preferred_element_type=F32)


def wide_left(a, b, ca, cb):
    high, low = halves(a)
    return dot(high, b, ca, cb) + dot(low, b, ca, cb)


def wide_right(a, b, ca, cb):
    high, low = halves(b)
    return dot(a, high, ca, cb) + dot(a, low, ca, cb)


def wide_both(a, b, ca, cb):
    ah, al = halves(a)
    bh, bl = halves(b)
    return dot(ah, bh, ca, cb) + (dot(ah, bl, ca, cb) + dot(al, bh, ca, cb))


def decay_between(col, row, diagonal):
    weight = jnp.exp(jnp.minimum(col - row, 0.0))
    if diagonal:
        shape = weight.shape
        lower = lax.broadcasted_iota(jnp.int32, shape, 0) >= lax.broadcasted_iota(jnp.int32, shape, 1)
        weight = jnp.where(lower, weight, 0.0)
    return weight


def state_kernel(k_ref, v_ref, col_ref, state_ref):
    col = col_ref[0]
    total = col[-1:, :]
    state_ref[0] = wide_right(k_ref[...], jnp.exp(total - col) * v_ref[...].astype(F32), 0, 0)


def forward_kernel(q_ref, k_ref, v_ref, col_ref, row_ref, state_ref, att_ref, normed_ref):
    rows = q_ref.shape[0]
    state = state_ref[0]
    for t in range(0, rows, SUB):
        query = q_ref[t : t + SUB, :]
        col = col_ref[0, t : t + SUB, :]
        total = jnp.exp(col) * wide_right(query, state, 1, 0)
        for s in range(0, t + 1, SUB):
            weight = decay_between(col, row_ref[0, :, s : s + SUB], s == t)
            scores = dot(query, k_ref[s : s + SUB, :], 1, 1) * weight
            total = total + wide_left(scores, v_ref[s : s + SUB, :], 1, 0)
        att_ref[t : t + SUB, :] = total
        scale = jnp.sqrt(jnp.mean(total * total, axis=-1, keepdims=True) + EPS)
        normed_ref[t : t + SUB, :] = (total / scale).astype(BF16)


def cotangent_kernel(q_ref, col_ref, att_ref, gn_ref, ga_ref, grad_ref):
    att = att_ref[...]
    scale = jnp.sqrt(jnp.mean(att * att, axis=-1, keepdims=True) + EPS)
    o_hat = att / scale
    gn = gn_ref[...]
    ga = (gn - o_hat * jnp.mean(gn * o_hat, axis=-1, keepdims=True)) / scale
    ga_ref[...] = ga
    grad_ref[0] = wide_right(q_ref[...], jnp.exp(col_ref[0]) * ga, 0, 0)


def backward_kernel(
    q_ref, k_ref, v_ref, ga_ref, col_ref, row_ref, state_ref, end_ref, gq_ref, gk_ref, gv_ref
):
    rows = q_ref.shape[0]
    state = state_ref[0]
    end = end_ref[0]
    col_all = col_ref[0]
    into_end = jnp.exp(col_all[-1:, :] - col_all)
    starts = range(0, rows, SUB)
    gk = {}
    gv = {}
    for s in starts:
        tail = into_end[s : s + SUB, :]
        gk[s] = tail * wide_right(v_ref[s : s + SUB, :], end, 1, 1)
        gv[s] = tail * wide_right(k_ref[s : s + SUB, :], end, 1, 0)
    for t in starts:
        query = q_ref[t : t + SUB, :]
        ga = ga_ref[t : t + SUB, :]
        col = col_all[t : t + SUB, :]
        gq = jnp.exp(col) * wide_both(ga, state, 1, 1)
        for s in range(0, t + 1, SUB):
            key = k_ref[s : s + SUB, :]
            weight = decay_between(col, row_ref[0, :, s : s + SUB], s == t)
            scores = dot(query, key, 1, 1) * weight
            mix = wide_left(ga, v_ref[s : s + SUB, :], 1, 1) * weight
            gq = gq + wide_left(mix, key, 1, 0)
            gk[s] = gk[s] + wide_left(mix, query, 0, 0)
            gv[s] = gv[s] + wide_both(scores, ga, 0, 0)
        gq_ref[t : t + SUB, :] = gq.astype(BF16)
    for s in starts:
        gk_ref[s : s + SUB, :] = gk[s].astype(BF16)
        gv_ref[s : s + SUB, :] = gv[s].astype(BF16)


def per_head(kernel, heads, rows, size, ins, outs, flops):
    kinds = {
        "tok": pl.BlockSpec((rows, size), lambda h: (0, h)),
        "col": pl.BlockSpec((1, rows, 1), lambda h: (h, 0, 0)),
        "row": pl.BlockSpec((1, 1, rows), lambda h: (h, 0, 0)),
        "state": pl.BlockSpec((1, size, size), lambda h: (h, 0, 0)),
    }
    shapes = {"tok": (rows, heads * size), "state": (heads, size, size)}
    return pl.pallas_call(
        kernel,
        grid=(heads,),
        in_specs=[kinds[kind] for kind in ins],
        out_specs=[kinds[kind] for kind, _ in outs],
        out_shape=[jax.ShapeDtypeStruct(shapes[kind], dtype) for kind, dtype in outs],
        compiler_params=pltpu.CompilerParams(vmem_limit_bytes=32 * 2**20),
        cost_estimate=pl.CostEstimate(
            flops=flops, bytes_accessed=4 * rows * heads * size * 2, transcendentals=0
        ),
    )


def seq_permute(x, send):
    count = lax.axis_size("seq")
    pairs = [(i, send(i)) for i in range(count)]
    return lax.ppermute(x, "seq", [(i, to) for i, to in pairs if 0 <= to < count])


def tp_blocks(x):
    count, mine = lax.axis_size("tp"), lax.axis_index("tp")
    blocks = []
    for hop in range(count // 2):
        block = x
        if hop:
            block = lax.ppermute(x, "tp", [(i, (i + 2 * hop) % count) for i in range(count)])
        place = lax.rem(mine + count - 2 * hop, count)
        blocks.append((place, block))
        other = place + 1 - 2 * lax.rem(place, 2)
        blocks.append((other, lax.ppermute(block, "tp", [(i, i ^ 1) for i in range(count)])))
    return blocks


def carried_in(log, state, backward):
    heads, size, _ = state.shape
    count, mine = lax.axis_size("seq"), lax.axis_index("seq")
    side = lax.rem(mine, 2)
    near = (side == 0) if backward else (side == 1)

    def packed(log, state):
        return jnp.concatenate(
            [state, jnp.broadcast_to(log[:, None, None], (heads, 8, size))], axis=1
        )

    def split(pack):
        return pack[:, size, 0], pack[:, :size, :]

    def decayed(log, state):
        return jnp.exp(log)[:, None, None] * state

    pair_log, pair_state = split(seq_permute(packed(log, state), lambda i: i ^ 1))
    both = jnp.where(near, decayed(log, pair_state) + state, decayed(pair_log, state) + pair_state)
    mine_pack = packed(log + pair_log, both)
    total = jnp.zeros_like(state)
    passed = jnp.zeros_like(log)
    for hop in range(1, count // 2):
        step = -2 * hop if backward else 2 * hop
        far_log, far_state = split(seq_permute(mine_pack, lambda i: i + step))
        total = total + decayed(passed, far_state)
        passed = passed + far_log
    return jnp.where(near, decayed(pair_log, total) + pair_state, total)


def prefix(log_decay):
    rows = log_decay.shape[0]
    upto = jnp.tril(jnp.ones((rows, rows), F32))
    return lax.dot_general(
        log_decay, upto, (((0,), (1,)), ((), ())), precision=lax.Precision.HIGHEST, preferred_element_type=F32
    )


def on_device_any(queries, keys, values, log_decay, out_weight, grad_out):
    rows, heads = log_decay.shape
    size = queries.shape[1] // heads
    count, mine = lax.axis_size("seq"), lax.axis_index("seq")
    tps = lax.axis_size("tp")

    weight_all = lax.all_gather(out_weight, "seq", axis=1, tiled=True)
    cotangent = tp_blocks(grad_out)

    cumul = prefix(log_decay)
    row = cumul[:, None, :]
    col = cumul[:, :, None]
    dev_log = cumul[:, -1]
    unit = 2 * rows * heads * size * size
    (dev_state,) = per_head(
        state_kernel, heads, rows, size, ("tok", "tok", "col"), (("state", F32),), 2 * unit
    )(keys, values, col)
    state_in = carried_in(dev_log, dev_state, False)

    grad_out, state_in = lax.optimization_barrier((grad_out, state_in))
    share = count // tps
    width = grad_out.shape[1] // share
    arrived = jnp.zeros((share, rows, width), grad_out.dtype)
    for turn in range(share):
        pairs = []
        for i in range(count):
            for j in range(tps):
                to = (share * j + (i % share + turn) % share) * tps + i // share
                pairs.append((i * tps + j, to))
        block = lax.rem(lax.rem(mine, share) + turn, share)
        piece = lax.dynamic_slice_in_dim(grad_out, block * width, width, axis=1)
        piece = lax.ppermute(piece, ("seq", "tp"), pairs)
        slot = lax.rem(lax.rem(mine, share) + share - turn, share)
        arrived = lax.dynamic_update_slice_in_dim(arrived, piece[None], slot, axis=0)
    by_columns = tp_blocks(arrived.reshape(share * rows, width))

    attended, normed = per_head(
        forward_kernel,
        heads,
        rows,
        size,
        ("tok", "tok", "tok", "col", "row", "state"),
        (("tok", F32), ("tok", BF16)),
        12 * unit,
    )(queries, keys, values, col, row, state_in)
    own_cot, own_columns = [cotangent[0][1]], [by_columns[0][1]]
    normed, weight_all, late_cot, late_columns = lax.optimization_barrier(
        (
            normed,
            weight_all,
            [block for _, block in cotangent[1:]],
            [block for _, block in by_columns[1:]],
        )
    )
    cotangent = [(at, x) for (at, _), x in zip(cotangent, own_cot + late_cot)]
    by_columns = [(at, x) for (at, _), x in zip(by_columns, own_columns + late_columns)]
    normed_all = lax.all_gather(normed, "seq", axis=0, tiled=True)

    grad_normed = jnp.zeros((rows, heads * size), F32)
    for place, block in cotangent:
        part = lax.dynamic_slice_in_dim(weight_all, place * share * width, share * width, axis=1)
        grad_normed = grad_normed + lax.dot_general(
            block, part, (((1,), (1,)), ((), ())), preferred_element_type=F32
        )
    grad_att, dev_grad = per_head(
        cotangent_kernel,
        heads,
        rows,
        size,
        ("tok", "col", "tok", "tok"),
        (("tok", F32), ("state", F32)),
        2 * unit,
    )(queries, col, attended, grad_normed)
    end_grad = carried_in(dev_log, dev_grad, True)
    grad_q, grad_k, grad_v = per_head(
        backward_kernel,
        heads,
        rows,
        size,
        ("tok", "tok", "tok", "tok", "col", "row", "state", "state"),
        (("tok", BF16), ("tok", BF16), ("tok", BF16)),
        40 * unit,
    )(queries, keys, values, grad_att, col, row, state_in, end_grad)
    grad_weight = jnp.zeros((width, heads * size), F32)
    for place, block in by_columns:
        part = lax.dynamic_slice_in_dim(normed_all, place * share * rows, share * rows, axis=0)
        grad_weight = grad_weight + lax.dot_general(
            block, part, (((0,), (0,)), ((), ())), preferred_element_type=F32
        )
    return grad_q, grad_k, grad_v, grad_weight


MESH = pl.DeviceIdType.MESH
ZS = 4
TPS = 4
CHUNKS = 4


def fused_kernel(
    q_in, k_in, v_in, w_in, g_in, col_ref, row_ref,
    gq_out, gk_out, gv_out, dw_out,
    q_ref, k_ref, v_ref, g1, wb, nb, att, gn, xs, xr, go,
    sl, px, zin, zout, si, gl, bx, bin_, bout, ds, dr, do, dw,
    loc, g_recv, gs1, gs2, gs3, w_recv, w_send,
    n_recv, n_send, x_send, x_recv, go_send, gn_recv, sx_send, sx_recv, zc_send, zc_recv,
    bx_send, bx_recv, bz_send, bz_recv, d_send, d_recv, do_send, dw_recv, st, dst,
):
    rows, columns = q_ref.shape
    heads, _, size = si.shape
    width = w_in.shape[1]
    per = heads // CHUNKS
    wide = per * size
    seq, tp = lax.axis_index("seq"), lax.axis_index("tp")
    z, x = lax.div(seq, 2), lax.rem(seq, 2)
    y, core = lax.div(tp, 2), lax.rem(tp, 2)
    inside = lax.rem(lax.div(z + 1, 2), 2)
    inner, outer = inside == 1, inside == 0
    i_z = 1 + lax.div(z, 2)
    o_z = 3 * lax.div(z, 2)
    mid, far = 3 - i_z, 3 - o_z
    part = i_z + o_z - z
    other_x = 1 - x
    tp_y, tp_s, tp_d = (1 - y) * 2 + core, y * 2 + 1 - core, (1 - y) * 2 + 1 - core

    def at(zz, xx, tt):
        return (zz * 2 + xx, tt)

    here_x = at(z, other_x, tp)
    here_y = at(z, x, tp_y)
    here_s = at(z, x, tp_s)

    def copy(src, dst, send, recv, to):
        return pltpu.make_async_remote_copy(
            src_ref=src, dst_ref=dst, send_sem=send, recv_sem=recv, device_id=to, device_id_type=MESH
        )

    ends = []

    def go_copy(c, when=None):
        ends.append((c, when))
        if when is None:
            c.start()
        else:
            pl.when(when)(c.start)

    barrier = pltpu.get_barrier_semaphore()
    peers = [at(lax.rem(z + d, ZS), x, tp) for d in range(1, ZS)]
    peers += [here_x, at(part, other_x, tp), here_y, here_s]
    for peer in peers:
        pl.semaphore_signal(barrier, inc=1, device_id=peer, device_id_type=MESH)
    pl.semaphore_wait(barrier, len(peers))

    def columns_of(h):
        return pl.ds(pl.multiple_of(h * size, size), size)

    def half(n):
        return g_in.at[:, pl.ds(pl.multiple_of(n * width, width), width)]

    def chunks(body, start=0, stop=CHUNKS):
        def step(n, _):
            body(n)
            return 0

        lax.fori_loop(start, stop, step, 0)

    def row_blocks(body):
        def step(r, _):
            body(r)
            return 0

        lax.fori_loop(0, rows // SUB, step, 0)

    def heads_of(n, body):
        def one(j, _):
            body(n * per + j, j)
            return 0

        lax.fori_loop(0, per, one, 0)

    def w_send_own(n, when=None):
        at_n = pl.ds(n * wide, wide)
        go_copy(copy(w_in.at[at_n], wb.at[z, at_n], w_send.at[0, n], w_recv.at[z, n], at(i_z + inside * (mid - i_z), x, tp)), when)

    def w_copy(src, n):
        at_n = pl.ds(n * wide, wide)
        return copy(wb.at[src, at_n], wb.at[src, at_n], w_send.at[1, n], w_recv.at[src, n], at(mid, x, tp))

    def w_relay(n):
        w_copy(part, n).wait_recv()
        w_copy(part, n).start()

    def g_got(s, t):
        return copy(g1.at[s, t], g1.at[s, t], gs3.at[s], g_recv.at[s, t], here_s)

    def spread(s, wait=None):
        pl.when(inner)(g_got(s, tp).wait_recv if wait is None else wait)
        for n, to in enumerate((here_y, here_s)):
            go_copy(copy(g1.at[s, tp], g1.at[s, tp], gs2.at[s, n], g_recv.at[s, tp], to), inner)

    def pass_on(s):
        pl.when(inner)(g_got(s, tp_y).wait_recv)
        go_copy(g_got(s, tp_y), inner)

    def rest_of(s):
        for t in (tp_s, tp_d):
            g_got(s, t).wait_recv()

    def local_state(h, j):
        col = col_ref[h]
        total = col[-1:, :]
        at_h = columns_of(h)
        sl[h, 0:size, :] = wide_right(k_ref[:, at_h], jnp.exp(total - col) * v_ref[:, at_h].astype(F32), 0, 0)
        sl[h, size:, :] = jnp.broadcast_to(total, (8, size))

    def chain(n, have, forward):
        mine, pair, came, leaves, result = (sl, px, zin, zout, si) if forward else (gl, bx, bin_, bout, gl)

        def one(h, j):
            log_own, log_pair = sl[h, size : size + 1, :], px[h, size : size + 1, :]
            own, other = mine[h, 0:size, :], pair[h, 0:size, :]
            near = (x == 1) if forward else (x == 0)
            both = jnp.where(near, jnp.exp(log_own) * other + own, jnp.exp(log_pair) * own + other)
            if have:
                total = came[h]
                leaves[h] = jnp.exp(log_own + log_pair) * total + both
                result[h] = jnp.where(near, jnp.exp(log_pair) * total + other, total)
            else:
                leaves[h] = both
                result[h] = jnp.where(near, other, jnp.zeros_like(other))

        heads_of(n, one)

    def sx_copy(n):
        at_n = pl.ds(n * per, per)
        return copy(sl.at[at_n], px.at[at_n], sx_send.at[n], sx_recv.at[n], here_x)

    def z_send(n):
        at_n = pl.ds(n * per, per)
        return copy(zout.at[at_n], zin.at[at_n], zc_send.at[n], zc_recv.at[n], at(lax.rem(z + 1, ZS), x, tp))

    def b_send(n):
        at_n = pl.ds(n * per, per)
        return copy(bout.at[at_n], bin_.at[at_n], bz_send.at[n], bz_recv.at[n], at(lax.rem(z + 3, ZS), x, tp))

    def bx_copy(n):
        at_n = pl.ds(n * per, per)
        return copy(gl.at[at_n], bx.at[at_n], bx_send.at[n], bx_recv.at[n], here_x)

    def n_near(n):
        return copy(nb.at[0, n], nb.at[2, n], n_send.at[0, n], n_recv.at[2, n], at(i_z, x, tp))

    def n_other(n):
        s = 3 - 2 * inside
        return copy(nb.at[0, n], nb.at[s, n], n_send.at[1, n], n_recv.at[s, n], at(i_z, other_x, tp))

    def n_got(s, n):
        return copy(nb.at[s, n], nb.at[s, n], n_send.at[1, n], n_recv.at[s, n], here_x)

    def forward(n):
        def one(h, j):
            at_h = columns_of(h)
            state = si[h]
            for t in range(0, rows, SUB):
                query = q_ref[t : t + SUB, at_h]
                col = col_ref[h, t : t + SUB, :]
                total = jnp.exp(col) * wide_right(query, state, 1, 0)
                for s in range(0, t + 1, SUB):
                    weight = decay_between(col, row_ref[h, :, s : s + SUB], s == t)
                    scores = dot(query, k_ref[s : s + SUB, at_h], 1, 1) * weight
                    total = total + wide_left(scores, v_ref[s : s + SUB, at_h], 1, 0)
                att[t : t + SUB, at_h] = total
                scale = jnp.sqrt(jnp.mean(total * total, axis=-1, keepdims=True) + EPS)
                nb[0, n, columns_of(j), t : t + SUB] = (total / scale).T.astype(BF16)

        heads_of(n, one)

    def product(s, n, r):
        total = None
        for t in range(TPS):
            one = dot(g1[s, t, pl.ds(r * SUB, SUB), :], wb[t, pl.ds(n * wide, wide), :], 1, 1)
            total = one if total is None else total + one
        return total

    def x_copy(n, k):
        return copy(xs.at[n, k], xr.at[n, k], x_send.at[n, k], x_recv.at[n, k], here_x)

    def go_out(n):
        return copy(go.at[n], gn.at[n], go_send.at[n], gn_recv.at[n], at(part, x, tp))

    def far_set(n, k):
        s = 1 + 2 * k

        @row_blocks
        def _(r):
            xs[n, k, pl.ds(r * SUB, SUB), :] = product(s, n, r).astype(BF16)

        x_copy(n, k).start()

    def near_set(n, k):
        s = 2 * k
        x_copy(n, k).wait_recv()

        @row_blocks
        def _(r):
            at_r = pl.ds(r * SUB, SUB)
            total = product(s, n, r) + xr[n, k, at_r, :].astype(F32)

            @pl.when(k == 0)
            def _():
                gn[n, at_r, :] = total

            @pl.when(k == 1)
            def _():
                go[n, at_r, :] = total

        pl.when(k == 1)(go_out(n).start)

    def cotangent(n):
        def one(h, j):
            at_h, at_j = columns_of(h), columns_of(j)
            a = att[:, at_h]
            scale = jnp.sqrt(jnp.mean(a * a, axis=-1, keepdims=True) + EPS)
            o_hat = a / scale
            g = gn[n, :, at_j]
            ga = (g - o_hat * jnp.mean(g * o_hat, axis=-1, keepdims=True)) / scale
            gn[n, :, at_j] = ga
            gl[h] = wide_right(q_ref[:, at_h], jnp.exp(col_ref[h]) * ga, 0, 0)

        heads_of(n, one)
        bx_copy(n).start()

    def end_state(n):
        bx_copy(n).wait()

        @pl.when(z == ZS - 1)
        def _():
            chain(n, False, False)

        @pl.when(z < ZS - 1)
        def _():
            b_send(n).wait_recv()
            chain(n, True, False)

        pl.when(z > 0)(b_send(n).start)

    stores = [
        pltpu.make_async_copy(dw.at[n], dw_out.at[pl.ds(n * wide, wide)], dst.at[n]) for n in range(CHUNKS)
    ]

    def out_copies(n):
        at_n = pl.ds(pl.multiple_of(n * wide, wide), wide)
        return [
            pltpu.make_async_copy(a.at[:, at_n], b.at[:, at_n], st.at[i, n])
            for i, (a, b) in enumerate(((q_ref, gq_out), (k_ref, gk_out), (v_ref, gv_out)))
        ]

    def backward(n):
        def one(h, j):
            at_h, at_j = columns_of(h), columns_of(j)
            state, end = si[h], gl[h]
            col_all = col_ref[h]
            into_end = jnp.exp(col_all[-1:, :] - col_all)
            starts = range(0, rows, SUB)
            gk, gv, gq = {}, {}, {}
            for s in starts:
                tail = into_end[s : s + SUB, :]
                gk[s] = tail * wide_right(v_ref[s : s + SUB, at_h], end, 1, 1)
                gv[s] = tail * wide_right(k_ref[s : s + SUB, at_h], end, 1, 0)
            for t in starts:
                query = q_ref[t : t + SUB, at_h]
                ga = gn[n, t : t + SUB, at_j]
                col = col_all[t : t + SUB, :]
                gq[t] = jnp.exp(col) * wide_both(ga, state, 1, 1)
                for s in range(0, t + 1, SUB):
                    key = k_ref[s : s + SUB, at_h]
                    weight = decay_between(col, row_ref[h, :, s : s + SUB], s == t)
                    scores = dot(query, key, 1, 1) * weight
                    mix = wide_left(ga, v_ref[s : s + SUB, at_h], 1, 1) * weight
                    gq[t] = gq[t] + wide_left(mix, key, 1, 0)
                    gk[s] = gk[s] + wide_left(mix, query, 0, 0)
                    gv[s] = gv[s] + wide_both(scores, ga, 0, 0)
            for s in starts:
                q_ref[s : s + SUB, at_h] = gq[s].astype(BF16)
                k_ref[s : s + SUB, at_h] = gk[s].astype(BF16)
                v_ref[s : s + SUB, at_h] = gv[s].astype(BF16)

        heads_of(n, one)
        for c in out_copies(n):
            c.start()

    def weight_product(b, n, m):
        total = None
        for s in range(4):
            one = dot(nb[s, n], g1[s, b, :, pl.ds(pl.multiple_of(m * SUB, SUB), SUB)], 1, 0)
            total = one if total is None else total + one
        return total

    def width_blocks(body):
        def step(m, _):
            body(m)
            return 0

        lax.fori_loop(0, width // SUB, step, 0)

    def d_copy(n, k):
        return copy(ds.at[n, k], dr.at[n, k], d_send.at[n, k], d_recv.at[n, k], at(mid, x, tp))

    def do_copy(n):
        return copy(do.at[n], do.at[n], do_send.at[n], dw_recv.at[n], at(part, x, tp))

    def weight_far(n):
        for s in (1, 2, 3):
            n_got(s, n).wait_recv()
        for k, b in enumerate((far, mid)):

            @width_blocks
            def _(m):
                ds[n, k, :, pl.ds(pl.multiple_of(m * SUB, SUB), SUB)] = weight_product(b, n, m).astype(BF16)

            d_copy(n, k).start()

    def weight_near(n, k):
        to, b = ((do, part), (dw, z))[k]
        d_copy(n, k).wait_recv()

        @width_blocks
        def _(m):
            at_m = pl.ds(pl.multiple_of(m * SUB, SUB), SUB)
            to[n, :, at_m] = (weight_product(b, n, m) + dr[n, k, :, at_m].astype(F32)).astype(to.dtype)

        if k == 0:
            do_copy(n).start()

    first, last, front, rear = z == 0, z == ZS - 1, z == 1, z == 2
    k_0, k_1 = 1, 0
    order = (3, 2, 1, 0)
    loads = [
        pltpu.make_async_copy(a, b, loc.at[n])
        for n, (a, b) in enumerate(((q_in, q_ref), (k_in, k_ref), (v_in, v_ref)))
    ]
    own_g = pltpu.make_async_copy(half(x), g1.at[0, tp], g_recv.at[0, tp])
    own_w = pltpu.make_async_copy(w_in, wb.at[z], loc.at[4])
    for c in loads[1:]:
        c.start()
    to_other = copy(half(other_x), g1.at[3 - 2 * inside, tp], gs1.at[0], g_recv.at[3 - 2 * inside, tp], at(i_z, other_x, tp))
    to_near = copy(half(x), g1.at[2, tp], gs1.at[1], g_recv.at[2, tp], at(i_z, x, tp))
    pl.when(outer)(to_other.start)
    pl.when(last)(to_near.start)
    for n in range(CHUNKS):
        w_send_own(n, (z > 0) if n < 2 else (z > 1))
    pl.when(inner)(own_g.start)
    pl.when(inner)(own_w.start)
    loads[0].start()
    for c in loads[1:]:
        c.wait()

    @chunks
    def _(n):
        heads_of(n, local_state)
        sx_copy(n).start()

    pl.when(inner)(to_other.start)

    @pl.when(first)
    def _():
        @chunks
        def _(n):
            sx_copy(n).wait_recv()
            chain(n, False, True)
            z_send(n).start()

    pl.when(first)(to_near.start)
    for n in range(CHUNKS):
        w_send_own(n, first)
    spread(order[0])

    @pl.when(z > 0)
    def _():
        @chunks
        def _(n):
            sx_copy(n).wait_recv()
            z_send(n).wait_recv()
            chain(n, True, True)
            pl.when(z < ZS - 1)(z_send(n).start)

    w_send_own(2, front)
    w_send_own(3, front)
    spread(order[1])
    loads[0].wait()

    def forward_part(n):
        forward(n)
        pl.when(inner)(n_other(n).start)

    chunks(forward_part, 0, CHUNKS // 2)
    pass_on(order[0])
    chunks(forward_part, CHUNKS // 2, CHUNKS)

    @pl.when(outer)
    def _():
        @chunks
        def _(n):
            n_other(n).start()
            n_near(n).start()

    spread(order[2])
    pass_on(order[1])

    def far_step(n):
        w_copy(mid, n).wait_recv()
        w_copy(far, n).wait_recv()
        far_set(n, k_0)

    @pl.when(inner)
    def _():
        own_w.wait()
        w_relay(0)
        rest_of(1 + 2 * k_0)
        w_relay(1)
        far_step(0)
        rest_of(2 * k_0)

        @functools.partial(chunks, start=1, stop=CHUNKS - 1)
        def _(n):
            w_relay(n + 1)
            far_step(n)
            near_set(n - 1, k_0)

    spread(order[3])
    pass_on(order[2])

    @pl.when(inner)
    def _():
        far_step(CHUNKS - 1)
        near_set(CHUNKS - 2, k_0)
        near_set(CHUNKS - 1, k_0)
        rest_of(1 + 2 * k_1)

        @chunks
        def _(n):
            far_set(n, k_1)

    pass_on(order[3])

    @pl.when(inner)
    def _():
        rest_of(2 * k_1)

        @chunks
        def _(n):
            near_set(n, k_1)


    @pl.when(inner)
    def _():
        @chunks
        def _(n):
            cotangent(n)
            weight_far(n)
            pl.when(n > 1)(lambda: weight_near(n - 2, 0))

    def tail_step(n):
        @pl.when(outer & (n < CHUNKS))
        def _():
            go_out(n).wait_recv()
            cotangent(n)

        @pl.when(n > 0)
        def _():
            end_state(n - 1)
            backward(n - 1)

        pl.when(inner & (n > 0) & (n < 3))(lambda: weight_near(n + 1, 0))

    chunks(tail_step, 0, CHUNKS + 1)

    @pl.when(inner)
    def _():
        chunks(lambda n: weight_near(n, 1))

    @pl.when(outer)
    def _():
        @chunks
        def _(n):
            do_copy(n).wait_recv()
            dw[n] = do[n].astype(F32)

    for c in stores:
        c.start()

    for c, when in ends:
        if when is None:
            c.wait_send()
        else:
            pl.when(when)(c.wait_send)
    to_other.wait_send()
    pl.when(outer)(to_near.wait_send)

    @chunks
    def _(n):
        sx_copy(n).wait_send()
        pl.when(z < ZS - 1)(z_send(n).wait_send)
        pl.when(z > 0)(b_send(n).wait_send)
        n_other(n).wait_send()
        pl.when(outer)(n_near(n).wait_send)

        @pl.when(inner)
        def _():
            w_copy(part, n).wait_send()
            d_copy(n, 0).wait_send()
            d_copy(n, 1).wait_send()
            do_copy(n).wait_send()
            x_copy(n, 0).wait_send()
            x_copy(n, 1).wait_send()
            go_out(n).wait_send()

        for c in out_copies(n):
            c.wait()

    for c in stores:
        c.wait()


def on_device(queries, keys, values, log_decay, out_weight, grad_out):
    rows, heads = log_decay.shape
    columns = queries.shape[1]
    size = columns // heads
    width = out_weight.shape[1]
    wide = columns // CHUNKS
    cumul = prefix(log_decay)
    dma = pltpu.SemaphoreType.DMA
    state = pltpu.VMEM((heads, size, size), F32)
    packed = pltpu.VMEM((heads, size + 8, size), F32)
    tokens = pltpu.VMEM((rows, columns), BF16)
    scratch = [
        tokens, tokens, tokens,
        pltpu.VMEM((4, TPS, rows, width), BF16),
        pltpu.VMEM((ZS, columns, width), BF16),
        pltpu.VMEM((4, CHUNKS, wide, rows), BF16),
        pltpu.VMEM((rows, columns), F32),
        pltpu.VMEM((CHUNKS, rows, wide), F32),
        pltpu.VMEM((CHUNKS, 2, rows, wide), BF16),
        pltpu.VMEM((CHUNKS, 2, rows, wide), BF16),
        pltpu.VMEM((CHUNKS, rows, wide), F32),
        packed, packed, state, state, state, state, state, state, state,
        pltpu.VMEM((CHUNKS, 2, wide, width), BF16),
        pltpu.VMEM((CHUNKS, 2, wide, width), BF16),
        pltpu.VMEM((CHUNKS, wide, width), BF16),
        pltpu.VMEM((CHUNKS, wide, width), F32),
        dma((8,)), dma((4, TPS)), dma((2,)), dma((4, 2)), dma((4,)),
        dma((ZS, CHUNKS)), dma((2, CHUNKS)),
        dma((4, CHUNKS)), dma((2, CHUNKS)), dma((CHUNKS, 2)), dma((CHUNKS, 2)), dma((CHUNKS,)), dma((CHUNKS,)),
        dma((CHUNKS,)), dma((CHUNKS,)), dma((CHUNKS,)), dma((CHUNKS,)),
        dma((CHUNKS,)), dma((CHUNKS,)), dma((CHUNKS,)), dma((CHUNKS,)), dma((CHUNKS, 2)), dma((CHUNKS, 2)),
        dma((CHUNKS,)), dma((CHUNKS,)), dma((3, CHUNKS)), dma((CHUNKS,)),
    ]
    anywhere, vmem = pl.BlockSpec(memory_space=pl.ANY), pl.BlockSpec(memory_space=pltpu.VMEM)
    token = jax.ShapeDtypeStruct((rows, columns), BF16)
    grad_q, grad_k, grad_v, grad_w = pl.pallas_call(
        fused_kernel,
        in_specs=[anywhere] * 5 + [vmem, vmem],
        out_specs=[anywhere] * 4,
        out_shape=[token, token, token, jax.ShapeDtypeStruct((columns, width), F32)],
        scratch_shapes=scratch,
        compiler_params=pltpu.CompilerParams(
            collective_id=0, has_side_effects=True, vmem_limit_bytes=60 * 2**20
        ),
    )(queries, keys, values, out_weight, grad_out, cumul[:, :, None], cumul[:, None, :])
    return grad_q, grad_k, grad_v, grad_w.T


def solution(mesh):
    spec = P("seq", "tp")
    known = dict(mesh.shape) == {"seq": 2 * ZS, "tp": TPS}
    return jax.shard_map(
        on_device if known else on_device_any,
        mesh=mesh,
        in_specs=(spec, spec, spec, spec, P("tp", "seq"), spec),
        out_specs=(spec, spec, spec, spec),
        check_vma=False,
    )
```

```python
import functools

import jax
import jax.numpy as jnp
from jax import lax
from jax.experimental import pallas as pl
from jax.experimental.pallas import tpu as pltpu
from jax.sharding import PartitionSpec as P

SUB = 256
EPS = 1e-06
F32 = jnp.float32
BF16 = jnp.bfloat16


def halves(x):
    high = x.astype(BF16)
    return high, (x - high.astype(F32)).astype(BF16)


def dot(a, b, ca, cb):
    return lax.dot_general(a, b, (((ca,), (cb,)), ((), ())), preferred_element_type=F32)


def wide_left(a, b, ca, cb):
    high, low = halves(a)
    return dot(high, b, ca, cb) + dot(low, b, ca, cb)


def wide_right(a, b, ca, cb):
    high, low = halves(b)
    return dot(a, high, ca, cb) + dot(a, low, ca, cb)


def wide_both(a, b, ca, cb):
    ah, al = halves(a)
    bh, bl = halves(b)
    return dot(ah, bh, ca, cb) + (dot(ah, bl, ca, cb) + dot(al, bh, ca, cb))


def decay_between(col, row, diagonal):
    weight = jnp.exp(jnp.minimum(col - row, 0.0))
    if diagonal:
        shape = weight.shape
        lower = lax.broadcasted_iota(jnp.int32, shape, 0) >= lax.broadcasted_iota(jnp.int32, shape, 1)
        weight = jnp.where(lower, weight, 0.0)
    return weight


def state_kernel(k_ref, v_ref, col_ref, state_ref):
    col = col_ref[0]
    total = col[-1:, :]
    state_ref[0] = wide_right(k_ref[...], jnp.exp(total - col) * v_ref[...].astype(F32), 0, 0)


def forward_kernel(q_ref, k_ref, v_ref, col_ref, row_ref, state_ref, att_ref, normed_ref):
    rows = q_ref.shape[0]
    state = state_ref[0]
    for t in range(0, rows, SUB):
        query = q_ref[t : t + SUB, :]
        col = col_ref[0, t : t + SUB, :]
        total = jnp.exp(col) * wide_right(query, state, 1, 0)
        for s in range(0, t + 1, SUB):
            weight = decay_between(col, row_ref[0, :, s : s + SUB], s == t)
            scores = dot(query, k_ref[s : s + SUB, :], 1, 1) * weight
            total = total + wide_left(scores, v_ref[s : s + SUB, :], 1, 0)
        att_ref[t : t + SUB, :] = total
        scale = jnp.sqrt(jnp.mean(total * total, axis=-1, keepdims=True) + EPS)
        normed_ref[t : t + SUB, :] = (total / scale).astype(BF16)


def cotangent_kernel(q_ref, col_ref, att_ref, gn_ref, ga_ref, grad_ref):
    att = att_ref[...]
    scale = jnp.sqrt(jnp.mean(att * att, axis=-1, keepdims=True) + EPS)
    o_hat = att / scale
    gn = gn_ref[...]
    ga = (gn - o_hat * jnp.mean(gn * o_hat, axis=-1, keepdims=True)) / scale
    ga_ref[...] = ga
    grad_ref[0] = wide_right(q_ref[...], jnp.exp(col_ref[0]) * ga, 0, 0)


def backward_kernel(
    q_ref, k_ref, v_ref, ga_ref, col_ref, row_ref, state_ref, end_ref, gq_ref, gk_ref, gv_ref
):
    rows = q_ref.shape[0]
    state = state_ref[0]
    end = end_ref[0]
    col_all = col_ref[0]
    into_end = jnp.exp(col_all[-1:, :] - col_all)
    starts = range(0, rows, SUB)
    gk = {}
    gv = {}
    for s in starts:
        tail = into_end[s : s + SUB, :]
        gk[s] = tail * wide_right(v_ref[s : s + SUB, :], end, 1, 1)
        gv[s] = tail * wide_right(k_ref[s : s + SUB, :], end, 1, 0)
    for t in starts:
        query = q_ref[t : t + SUB, :]
        ga = ga_ref[t : t + SUB, :]
        col = col_all[t : t + SUB, :]
        gq = jnp.exp(col) * wide_both(ga, state, 1, 1)
        for s in range(0, t + 1, SUB):
            key = k_ref[s : s + SUB, :]
            weight = decay_between(col, row_ref[0, :, s : s + SUB], s == t)
            scores = dot(query, key, 1, 1) * weight
            mix = wide_left(ga, v_ref[s : s + SUB, :], 1, 1) * weight
            gq = gq + wide_left(mix, key, 1, 0)
            gk[s] = gk[s] + wide_left(mix, query, 0, 0)
            gv[s] = gv[s] + wide_both(scores, ga, 0, 0)
        gq_ref[t : t + SUB, :] = gq.astype(BF16)
    for s in starts:
        gk_ref[s : s + SUB, :] = gk[s].astype(BF16)
        gv_ref[s : s + SUB, :] = gv[s].astype(BF16)


def per_head(kernel, heads, rows, size, ins, outs, flops):
    kinds = {
        "tok": pl.BlockSpec((rows, size), lambda h: (0, h)),
        "col": pl.BlockSpec((1, rows, 1), lambda h: (h, 0, 0)),
        "row": pl.BlockSpec((1, 1, rows), lambda h: (h, 0, 0)),
        "state": pl.BlockSpec((1, size, size), lambda h: (h, 0, 0)),
    }
    shapes = {"tok": (rows, heads * size), "state": (heads, size, size)}
    return pl.pallas_call(
        kernel,
        grid=(heads,),
        in_specs=[kinds[kind] for kind in ins],
        out_specs=[kinds[kind] for kind, _ in outs],
        out_shape=[jax.ShapeDtypeStruct(shapes[kind], dtype) for kind, dtype in outs],
        compiler_params=pltpu.CompilerParams(vmem_limit_bytes=32 * 2**20),
        cost_estimate=pl.CostEstimate(
            flops=flops, bytes_accessed=4 * rows * heads * size * 2, transcendentals=0
        ),
    )


def seq_permute(x, send):
    count = lax.axis_size("seq")
    pairs = [(i, send(i)) for i in range(count)]
    return lax.ppermute(x, "seq", [(i, to) for i, to in pairs if 0 <= to < count])


def tp_blocks(x):
    count, mine = lax.axis_size("tp"), lax.axis_index("tp")
    blocks = []
    for hop in range(count // 2):
        block = x
        if hop:
            block = lax.ppermute(x, "tp", [(i, (i + 2 * hop) % count) for i in range(count)])
        place = lax.rem(mine + count - 2 * hop, count)
        blocks.append((place, block))
        other = place + 1 - 2 * lax.rem(place, 2)
        blocks.append((other, lax.ppermute(block, "tp", [(i, i ^ 1) for i in range(count)])))
    return blocks


def carried_in(log, state, backward):
    heads, size, _ = state.shape
    count, mine = lax.axis_size("seq"), lax.axis_index("seq")
    side = lax.rem(mine, 2)
    near = (side == 0) if backward else (side == 1)

    def packed(log, state):
        return jnp.concatenate(
            [state, jnp.broadcast_to(log[:, None, None], (heads, 8, size))], axis=1
        )

    def split(pack):
        return pack[:, size, 0], pack[:, :size, :]

    def decayed(log, state):
        return jnp.exp(log)[:, None, None] * state

    pair_log, pair_state = split(seq_permute(packed(log, state), lambda i: i ^ 1))
    both = jnp.where(near, decayed(log, pair_state) + state, decayed(pair_log, state) + pair_state)
    mine_pack = packed(log + pair_log, both)
    total = jnp.zeros_like(state)
    passed = jnp.zeros_like(log)
    for hop in range(1, count // 2):
        step = -2 * hop if backward else 2 * hop
        far_log, far_state = split(seq_permute(mine_pack, lambda i: i + step))
        total = total + decayed(passed, far_state)
        passed = passed + far_log
    return jnp.where(near, decayed(pair_log, total) + pair_state, total)


def prefix(log_decay):
    rows = log_decay.shape[0]
    upto = jnp.tril(jnp.ones((rows, rows), F32))
    return lax.dot_general(
        log_decay, upto, (((0,), (1,)), ((), ())), precision=lax.Precision.HIGHEST, preferred_element_type=F32
    )


def on_device_any(queries, keys, values, log_decay, out_weight, grad_out):
    rows, heads = log_decay.shape
    size = queries.shape[1] // heads
    count, mine = lax.axis_size("seq"), lax.axis_index("seq")
    tps = lax.axis_size("tp")

    weight_all = lax.all_gather(out_weight, "seq", axis=1, tiled=True)
    cotangent = tp_blocks(grad_out)

    cumul = prefix(log_decay)
    row = cumul[:, None, :]
    col = cumul[:, :, None]
    dev_log = cumul[:, -1]
    unit = 2 * rows * heads * size * size
    (dev_state,) = per_head(
        state_kernel, heads, rows, size, ("tok", "tok", "col"), (("state", F32),), 2 * unit
    )(keys, values, col)
    state_in = carried_in(dev_log, dev_state, False)

    grad_out, state_in = lax.optimization_barrier((grad_out, state_in))
    share = count // tps
    width = grad_out.shape[1] // share
    arrived = jnp.zeros((share, rows, width), grad_out.dtype)
    for turn in range(share):
        pairs = []
        for i in range(count):
            for j in range(tps):
                to = (share * j + (i % share + turn) % share) * tps + i // share
                pairs.append((i * tps + j, to))
        block = lax.rem(lax.rem(mine, share) + turn, share)
        piece = lax.dynamic_slice_in_dim(grad_out, block * width, width, axis=1)
        piece = lax.ppermute(piece, ("seq", "tp"), pairs)
        slot = lax.rem(lax.rem(mine, share) + share - turn, share)
        arrived = lax.dynamic_update_slice_in_dim(arrived, piece[None], slot, axis=0)
    by_columns = tp_blocks(arrived.reshape(share * rows, width))

    attended, normed = per_head(
        forward_kernel,
        heads,
        rows,
        size,
        ("tok", "tok", "tok", "col", "row", "state"),
        (("tok", F32), ("tok", BF16)),
        12 * unit,
    )(queries, keys, values, col, row, state_in)
    own_cot, own_columns = [cotangent[0][1]], [by_columns[0][1]]
    normed, weight_all, late_cot, late_columns = lax.optimization_barrier(
        (
            normed,
            weight_all,
            [block for _, block in cotangent[1:]],
            [block for _, block in by_columns[1:]],
        )
    )
    cotangent = [(at, x) for (at, _), x in zip(cotangent, own_cot + late_cot)]
    by_columns = [(at, x) for (at, _), x in zip(by_columns, own_columns + late_columns)]
    normed_all = lax.all_gather(normed, "seq", axis=0, tiled=True)

    grad_normed = jnp.zeros((rows, heads * size), F32)
    for place, block in cotangent:
        part = lax.dynamic_slice_in_dim(weight_all, place * share * width, share * width, axis=1)
        grad_normed = grad_normed + lax.dot_general(
            block, part, (((1,), (1,)), ((), ())), preferred_element_type=F32
        )
    grad_att, dev_grad = per_head(
        cotangent_kernel,
        heads,
        rows,
        size,
        ("tok", "col", "tok", "tok"),
        (("tok", F32), ("state", F32)),
        2 * unit,
    )(queries, col, attended, grad_normed)
    end_grad = carried_in(dev_log, dev_grad, True)
    grad_q, grad_k, grad_v = per_head(
        backward_kernel,
        heads,
        rows,
        size,
        ("tok", "tok", "tok", "tok", "col", "row", "state", "state"),
        (("tok", BF16), ("tok", BF16), ("tok", BF16)),
        40 * unit,
    )(queries, keys, values, grad_att, col, row, state_in, end_grad)
    grad_weight = jnp.zeros((width, heads * size), F32)
    for place, block in by_columns:
        part = lax.dynamic_slice_in_dim(normed_all, place * share * rows, share * rows, axis=0)
        grad_weight = grad_weight + lax.dot_general(
            block, part, (((0,), (0,)), ((), ())), preferred_element_type=F32
        )
    return grad_q, grad_k, grad_v, grad_weight


MESH = pl.DeviceIdType.MESH
ZS = 4
TPS = 4
CHUNKS = 4


def fused_kernel(
    q_in, k_in, v_in, w_in, g_in, col_ref, row_ref,
    gq_out, gk_out, gv_out, dw_out,
    q_ref, k_ref, v_ref, g1, wb, nb, att, gn, xs, xr, go,
    sl, px, zin, zout, si, gl, bx, bin_, bout, ds, dr, do, dw,
    loc, g_recv, gs1, gs2, gs3, w_recv, w_send,
    n_recv, n_send, x_send, x_recv, go_send, gn_recv, sx_send, sx_recv, zc_send, zc_recv,
    bx_send, bx_recv, bz_send, bz_recv, d_send, d_recv, do_send, dw_recv, st, dst,
):
    rows, columns = q_ref.shape
    heads, _, size = si.shape
    width = w_in.shape[1]
    per = heads // CHUNKS
    wide = per * size
    seq, tp = lax.axis_index("seq"), lax.axis_index("tp")
    z, x = lax.div(seq, 2), lax.rem(seq, 2)
    y, core = lax.div(tp, 2), lax.rem(tp, 2)
    inside = lax.rem(lax.div(z + 1, 2), 2)
    inner, outer = inside == 1, inside == 0
    i_z = 1 + lax.div(z, 2)
    o_z = 3 * lax.div(z, 2)
    mid, far = 3 - i_z, 3 - o_z
    part = i_z + o_z - z
    other_x = 1 - x
    tp_y, tp_s, tp_d = (1 - y) * 2 + core, y * 2 + 1 - core, (1 - y) * 2 + 1 - core

    def at(zz, xx, tt):
        return (zz * 2 + xx, tt)

    here_x = at(z, other_x, tp)
    here_y = at(z, x, tp_y)
    here_s = at(z, x, tp_s)

    def copy(src, dst, send, recv, to):
        return pltpu.make_async_remote_copy(
            src_ref=src, dst_ref=dst, send_sem=send, recv_sem=recv, device_id=to, device_id_type=MESH
        )

    ends = []

    def go_copy(c, when=None):
        ends.append((c, when))
        if when is None:
            c.start()
        else:
            pl.when(when)(c.start)

    barrier = pltpu.get_barrier_semaphore()
    peers = [at(lax.rem(z + d, ZS), x, tp) for d in range(1, ZS)]
    peers += [here_x, at(part, other_x, tp), here_y, here_s]
    for peer in peers:
        pl.semaphore_signal(barrier, inc=1, device_id=peer, device_id_type=MESH)
    pl.semaphore_wait(barrier, len(peers))

    def columns_of(h):
        return pl.ds(pl.multiple_of(h * size, size), size)

    def half(n):
        return g_in.at[:, pl.ds(pl.multiple_of(n * width, width), width)]

    def chunks(body, start=0, stop=CHUNKS):
        def step(n, _):
            body(n)
            return 0

        lax.fori_loop(start, stop, step, 0)

    def row_blocks(body):
        def step(r, _):
            body(r)
            return 0

        lax.fori_loop(0, rows // SUB, step, 0)

    def heads_of(n, body):
        def one(j, _):
            body(n * per + j, j)
            return 0

        lax.fori_loop(0, per, one, 0)

    def w_send_own(n, when=None):
        at_n = pl.ds(n * wide, wide)
        go_copy(copy(w_in.at[at_n], wb.at[z, at_n], w_send.at[0, n], w_recv.at[z, n], at(i_z + inside * (mid - i_z), x, tp)), when)

    def w_copy(src, n):
        at_n = pl.ds(n * wide, wide)
        return copy(wb.at[src, at_n], wb.at[src, at_n], w_send.at[1, n], w_recv.at[src, n], at(mid, x, tp))

    def w_relay(n):
        w_copy(part, n).wait_recv()
        w_copy(part, n).start()

    def g_got(s, t):
        return copy(g1.at[s, t], g1.at[s, t], gs3.at[s], g_recv.at[s, t], here_s)

    def spread(s, wait=None):
        pl.when(inner)(g_got(s, tp).wait_recv if wait is None else wait)
        for n, to in enumerate((here_y, here_s)):
            go_copy(copy(g1.at[s, tp], g1.at[s, tp], gs2.at[s, n], g_recv.at[s, tp], to), inner)

    def pass_on(s):
        pl.when(inner)(g_got(s, tp_y).wait_recv)
        go_copy(g_got(s, tp_y), inner)

    def rest_of(s):
        for t in (tp_s, tp_d):
            g_got(s, t).wait_recv()

    def local_state(h, j):
        col = col_ref[h]
        total = col[-1:, :]
        at_h = columns_of(h)
        sl[h, 0:size, :] = wide_right(k_ref[:, at_h], jnp.exp(total - col) * v_ref[:, at_h].astype(F32), 0, 0)
        sl[h, size:, :] = jnp.broadcast_to(total, (8, size))

    def chain(n, have, forward):
        mine, pair, came, leaves, result = (sl, px, zin, zout, si) if forward else (gl, bx, bin_, bout, gl)

        def one(h, j):
            log_own, log_pair = sl[h, size : size + 1, :], px[h, size : size + 1, :]
            own, other = mine[h, 0:size, :], pair[h, 0:size, :]
            near = (x == 1) if forward else (x == 0)
            both = jnp.where(near, jnp.exp(log_own) * other + own, jnp.exp(log_pair) * own + other)
            if have:
                total = came[h]
                leaves[h] = jnp.exp(log_own + log_pair) * total + both
                result[h] = jnp.where(near, jnp.exp(log_pair) * total + other, total)
            else:
                leaves[h] = both
                result[h] = jnp.where(near, other, jnp.zeros_like(other))

        heads_of(n, one)

    def sx_copy(n):
        at_n = pl.ds(n * per, per)
        return copy(sl.at[at_n], px.at[at_n], sx_send.at[n], sx_recv.at[n], here_x)

    def z_send(n):
        at_n = pl.ds(n * per, per)
        return copy(zout.at[at_n], zin.at[at_n], zc_send.at[n], zc_recv.at[n], at(lax.rem(z + 1, ZS), x, tp))

    def b_send(n):
        at_n = pl.ds(n * per, per)
        return copy(bout.at[at_n], bin_.at[at_n], bz_send.at[n], bz_recv.at[n], at(lax.rem(z + 3, ZS), x, tp))

    def bx_copy(n):
        at_n = pl.ds(n * per, per)
        return copy(gl.at[at_n], bx.at[at_n], bx_send.at[n], bx_recv.at[n], here_x)

    def n_near(n):
        return copy(nb.at[0, n], nb.at[2, n], n_send.at[0, n], n_recv.at[2, n], at(i_z, x, tp))

    def n_other(n):
        s = 3 - 2 * inside
        return copy(nb.at[0, n], nb.at[s, n], n_send.at[1, n], n_recv.at[s, n], at(i_z, other_x, tp))

    def n_got(s, n):
        return copy(nb.at[s, n], nb.at[s, n], n_send.at[1, n], n_recv.at[s, n], here_x)

    def forward(n):
        def one(h, j):
            at_h = columns_of(h)
            state = si[h]
            for t in range(0, rows, SUB):
                query = q_ref[t : t + SUB, at_h]
                col = col_ref[h, t : t + SUB, :]
                total = jnp.exp(col) * wide_right(query, state, 1, 0)
                for s in range(0, t + 1, SUB):
                    weight = decay_between(col, row_ref[h, :, s : s + SUB], s == t)
                    scores = dot(query, k_ref[s : s + SUB, at_h], 1, 1) * weight
                    total = total + wide_left(scores, v_ref[s : s + SUB, at_h], 1, 0)
                att[t : t + SUB, at_h] = total
                scale = jnp.sqrt(jnp.mean(total * total, axis=-1, keepdims=True) + EPS)
                nb[0, n, columns_of(j), t : t + SUB] = (total / scale).T.astype(BF16)

        heads_of(n, one)

    def product(s, n, r):
        total = None
        for t in range(TPS):
            one = dot(g1[s, t, pl.ds(r * SUB, SUB), :], wb[t, pl.ds(n * wide, wide), :], 1, 1)
            total = one if total is None else total + one
        return total

    def x_copy(n, k):
        return copy(xs.at[n, k], xr.at[n, k], x_send.at[n, k], x_recv.at[n, k], here_x)

    def go_out(n):
        return copy(go.at[n], gn.at[n], go_send.at[n], gn_recv.at[n], at(part, x, tp))

    def far_set(n, k):
        s = 1 + 2 * k

        @row_blocks
        def _(r):
            xs[n, k, pl.ds(r * SUB, SUB), :] = product(s, n, r).astype(BF16)

        x_copy(n, k).start()

    def near_set(n, k):
        s = 2 * k
        x_copy(n, k).wait_recv()

        @row_blocks
        def _(r):
            at_r = pl.ds(r * SUB, SUB)
            total = product(s, n, r) + xr[n, k, at_r, :].astype(F32)

            @pl.when(k == 0)
            def _():
                gn[n, at_r, :] = total

            @pl.when(k == 1)
            def _():
                go[n, at_r, :] = total

        pl.when(k == 1)(go_out(n).start)

    def cotangent(n):
        def one(h, j):
            at_h, at_j = columns_of(h), columns_of(j)
            a = att[:, at_h]
            scale = jnp.sqrt(jnp.mean(a * a, axis=-1, keepdims=True) + EPS)
            o_hat = a / scale
            g = gn[n, :, at_j]
            ga = (g - o_hat * jnp.mean(g * o_hat, axis=-1, keepdims=True)) / scale
            gn[n, :, at_j] = ga
            gl[h] = wide_right(q_ref[:, at_h], jnp.exp(col_ref[h]) * ga, 0, 0)

        heads_of(n, one)
        bx_copy(n).start()

    def end_state(n):
        bx_copy(n).wait()

        @pl.when(z == ZS - 1)
        def _():
            chain(n, False, False)

        @pl.when(z < ZS - 1)
        def _():
            b_send(n).wait_recv()
            chain(n, True, False)

        pl.when(z > 0)(b_send(n).start)

    stores = [
        pltpu.make_async_copy(dw.at[n], dw_out.at[pl.ds(n * wide, wide)], dst.at[n]) for n in range(CHUNKS)
    ]

    def out_copies(n):
        at_n = pl.ds(pl.multiple_of(n * wide, wide), wide)
        return [
            pltpu.make_async_copy(a.at[:, at_n], b.at[:, at_n], st.at[i, n])
            for i, (a, b) in enumerate(((q_ref, gq_out), (k_ref, gk_out), (v_ref, gv_out)))
        ]

    def backward(n):
        def one(h, j):
            at_h, at_j = columns_of(h), columns_of(j)
            state, end = si[h], gl[h]
            col_all = col_ref[h]
            into_end = jnp.exp(col_all[-1:, :] - col_all)
            starts = range(0, rows, SUB)
            gk, gv, gq = {}, {}, {}
            for s in starts:
                tail = into_end[s : s + SUB, :]
                gk[s] = tail * wide_right(v_ref[s : s + SUB, at_h], end, 1, 1)
                gv[s] = tail * wide_right(k_ref[s : s + SUB, at_h], end, 1, 0)
            for t in starts:
                query = q_ref[t : t + SUB, at_h]
                ga = gn[n, t : t + SUB, at_j]
                col = col_all[t : t + SUB, :]
                gq[t] = jnp.exp(col) * wide_both(ga, state, 1, 1)
                for s in range(0, t + 1, SUB):
                    key = k_ref[s : s + SUB, at_h]
                    weight = decay_between(col, row_ref[h, :, s : s + SUB], s == t)
                    scores = dot(query, key, 1, 1) * weight
                    mix = wide_left(ga, v_ref[s : s + SUB, at_h], 1, 1) * weight
                    gq[t] = gq[t] + wide_left(mix, key, 1, 0)
                    gk[s] = gk[s] + wide_left(mix, query, 0, 0)
                    gv[s] = gv[s] + wide_both(scores, ga, 0, 0)
            for s in starts:
                q_ref[s : s + SUB, at_h] = gq[s].astype(BF16)
                k_ref[s : s + SUB, at_h] = gk[s].astype(BF16)
                v_ref[s : s + SUB, at_h] = gv[s].astype(BF16)

        heads_of(n, one)
        for c in out_copies(n):
            c.start()

    def weight_product(b, n, m):
        total = None
        for s in range(4):
            one = dot(nb[s, n], g1[s, b, :, pl.ds(pl.multiple_of(m * SUB, SUB), SUB)], 1, 0)
            total = one if total is None else total + one
        return total

    def width_blocks(body):
        def step(m, _):
            body(m)
            return 0

        lax.fori_loop(0, width // SUB, step, 0)

    def d_copy(n, k):
        return copy(ds.at[n, k], dr.at[n, k], d_send.at[n, k], d_recv.at[n, k], at(mid, x, tp))

    def do_copy(n):
        return copy(do.at[n], do.at[n], do_send.at[n], dw_recv.at[n], at(part, x, tp))

    def weight_far(n):
        for s in (1, 2, 3):
            n_got(s, n).wait_recv()
        for k, b in enumerate((far, mid)):

            @width_blocks
            def _(m):
                ds[n, k, :, pl.ds(pl.multiple_of(m * SUB, SUB), SUB)] = weight_product(b, n, m).astype(BF16)

            d_copy(n, k).start()

    def weight_near(n, k):
        to, b = ((do, part), (dw, z))[k]
        d_copy(n, k).wait_recv()

        @width_blocks
        def _(m):
            at_m = pl.ds(pl.multiple_of(m * SUB, SUB), SUB)
            to[n, :, at_m] = (weight_product(b, n, m) + dr[n, k, :, at_m].astype(F32)).astype(to.dtype)

        if k == 0:
            do_copy(n).start()

    first, last, front, rear = z == 0, z == ZS - 1, z == 1, z == 2
    k_0, k_1 = 1, 0
    order = (3, 2, 1, 0)
    loads = [
        pltpu.make_async_copy(a, b, loc.at[n])
        for n, (a, b) in enumerate(((q_in, q_ref), (k_in, k_ref), (v_in, v_ref)))
    ]
    own_g = pltpu.make_async_copy(half(x), g1.at[0, tp], g_recv.at[0, tp])
    own_w = pltpu.make_async_copy(w_in, wb.at[z], loc.at[4])
    for c in loads[1:]:
        c.start()
    to_other = copy(half(other_x), g1.at[3 - 2 * inside, tp], gs1.at[0], g_recv.at[3 - 2 * inside, tp], at(i_z, other_x, tp))
    to_near = copy(half(x), g1.at[2, tp], gs1.at[1], g_recv.at[2, tp], at(i_z, x, tp))
    pl.when(outer)(to_other.start)
    pl.when(last)(to_near.start)
    for n in range(CHUNKS):
        w_send_own(n, (z > 0) if n < 2 else (z > 1))
    pl.when(inner)(own_g.start)
    pl.when(inner)(own_w.start)
    loads[0].start()
    for c in loads[1:]:
        c.wait()

    @chunks
    def _(n):
        heads_of(n, local_state)
        sx_copy(n).start()

    pl.when(inner)(to_other.start)

    @pl.when(first)
    def _():
        @chunks
        def _(n):
            sx_copy(n).wait_recv()
            chain(n, False, True)
            z_send(n).start()

    pl.when(first)(to_near.start)
    for n in range(CHUNKS):
        w_send_own(n, first)
    spread(order[0])

    @pl.when(z > 0)
    def _():
        @chunks
        def _(n):
            sx_copy(n).wait_recv()
            z_send(n).wait_recv()
            chain(n, True, True)
            pl.when(z < ZS - 1)(z_send(n).start)

    w_send_own(2, front)
    w_send_own(3, front)
    spread(order[1])
    loads[0].wait()

    def forward_part(n):
        forward(n)
        pl.when(inner)(n_other(n).start)

    chunks(forward_part, 0, CHUNKS // 2)
    pass_on(order[0])
    chunks(forward_part, CHUNKS // 2, CHUNKS)

    @pl.when(outer)
    def _():
        @chunks
        def _(n):
            n_other(n).start()
            n_near(n).start()

    spread(order[2])
    pass_on(order[1])

    def far_step(n):
        w_copy(mid, n).wait_recv()
        w_copy(far, n).wait_recv()
        far_set(n, k_0)

    @pl.when(inner)
    def _():
        own_w.wait()
        w_relay(0)
        rest_of(1 + 2 * k_0)
        w_relay(1)
        far_step(0)
        rest_of(2 * k_0)

        @functools.partial(chunks, start=1, stop=CHUNKS - 1)
        def _(n):
            w_relay(n + 1)
            far_step(n)
            near_set(n - 1, k_0)

    spread(order[3])
    pass_on(order[2])

    @pl.when(inner)
    def _():
        far_step(CHUNKS - 1)
        near_set(CHUNKS - 2, k_0)
        near_set(CHUNKS - 1, k_0)
        rest_of(1 + 2 * k_1)

        @chunks
        def _(n):
            far_set(n, k_1)

    pass_on(order[3])

    @pl.when(inner)
    def _():
        rest_of(2 * k_1)
        chunks(weight_far)

        @chunks
        def _(n):
            near_set(n, k_1)


    @pl.when(inner)
    def _():
        @chunks
        def _(n):
            cotangent(n)
            pl.when(n < 2)(lambda: weight_near(n, 0))

    def tail_step(n):
        @pl.when(outer & (n < CHUNKS))
        def _():
            go_out(n).wait_recv()
            cotangent(n)

        @pl.when(n > 0)
        def _():
            end_state(n - 1)
            backward(n - 1)

        pl.when(inner & (n > 0) & (n < 3))(lambda: weight_near(n + 1, 0))

    chunks(tail_step, 0, CHUNKS + 1)

    @pl.when(inner)
    def _():
        chunks(lambda n: weight_near(n, 1))

    @pl.when(outer)
    def _():
        @chunks
        def _(n):
            do_copy(n).wait_recv()
            dw[n] = do[n].astype(F32)

    for c in stores:
        c.start()

    for c, when in ends:
        if when is None:
            c.wait_send()
        else:
            pl.when(when)(c.wait_send)
    to_other.wait_send()
    pl.when(outer)(to_near.wait_send)

    @chunks
    def _(n):
        sx_copy(n).wait_send()
        pl.when(z < ZS - 1)(z_send(n).wait_send)
        pl.when(z > 0)(b_send(n).wait_send)
        n_other(n).wait_send()
        pl.when(outer)(n_near(n).wait_send)

        @pl.when(inner)
        def _():
            w_copy(part, n).wait_send()
            d_copy(n, 0).wait_send()
            d_copy(n, 1).wait_send()
            do_copy(n).wait_send()
            x_copy(n, 0).wait_send()
            x_copy(n, 1).wait_send()
            go_out(n).wait_send()

        for c in out_copies(n):
            c.wait()

    for c in stores:
        c.wait()


def on_device(queries, keys, values, log_decay, out_weight, grad_out):
    rows, heads = log_decay.shape
    columns = queries.shape[1]
    size = columns // heads
    width = out_weight.shape[1]
    wide = columns // CHUNKS
    cumul = prefix(log_decay)
    dma = pltpu.SemaphoreType.DMA
    state = pltpu.VMEM((heads, size, size), F32)
    packed = pltpu.VMEM((heads, size + 8, size), F32)
    tokens = pltpu.VMEM((rows, columns), BF16)
    scratch = [
        tokens, tokens, tokens,
        pltpu.VMEM((4, TPS, rows, width), BF16),
        pltpu.VMEM((ZS, columns, width), BF16),
        pltpu.VMEM((4, CHUNKS, wide, rows), BF16),
        pltpu.VMEM((rows, columns), F32),
        pltpu.VMEM((CHUNKS, rows, wide), F32),
        pltpu.VMEM((CHUNKS, 2, rows, wide), BF16),
        pltpu.VMEM((CHUNKS, 2, rows, wide), BF16),
        pltpu.VMEM((CHUNKS, rows, wide), F32),
        packed, packed, state, state, state, state, state, state, state,
        pltpu.VMEM((CHUNKS, 2, wide, width), BF16),
        pltpu.VMEM((CHUNKS, 2, wide, width), BF16),
        pltpu.VMEM((CHUNKS, wide, width), BF16),
        pltpu.VMEM((CHUNKS, wide, width), F32),
        dma((8,)), dma((4, TPS)), dma((2,)), dma((4, 2)), dma((4,)),
        dma((ZS, CHUNKS)), dma((2, CHUNKS)),
        dma((4, CHUNKS)), dma((2, CHUNKS)), dma((CHUNKS, 2)), dma((CHUNKS, 2)), dma((CHUNKS,)), dma((CHUNKS,)),
        dma((CHUNKS,)), dma((CHUNKS,)), dma((CHUNKS,)), dma((CHUNKS,)),
        dma((CHUNKS,)), dma((CHUNKS,)), dma((CHUNKS,)), dma((CHUNKS,)), dma((CHUNKS, 2)), dma((CHUNKS, 2)),
        dma((CHUNKS,)), dma((CHUNKS,)), dma((3, CHUNKS)), dma((CHUNKS,)),
    ]
    anywhere, vmem = pl.BlockSpec(memory_space=pl.ANY), pl.BlockSpec(memory_space=pltpu.VMEM)
    token = jax.ShapeDtypeStruct((rows, columns), BF16)
    grad_q, grad_k, grad_v, grad_w = pl.pallas_call(
        fused_kernel,
        in_specs=[anywhere] * 5 + [vmem, vmem],
        out_specs=[anywhere] * 4,
        out_shape=[token, token, token, jax.ShapeDtypeStruct((columns, width), F32)],
        scratch_shapes=scratch,
        compiler_params=pltpu.CompilerParams(
            collective_id=0, has_side_effects=True, vmem_limit_bytes=60 * 2**20
        ),
    )(queries, keys, values, out_weight, grad_out, cumul[:, :, None], cumul[:, None, :])
    return grad_q, grad_k, grad_v, grad_w.T


def solution(mesh):
    spec = P("seq", "tp")
    known = dict(mesh.shape) == {"seq": 2 * ZS, "tp": TPS}
    return jax.shard_map(
        on_device if known else on_device_any,
        mesh=mesh,
        in_specs=(spec, spec, spec, spec, P("tp", "seq"), spec),
        out_specs=(spec, spec, spec, spec),
        check_vma=False,
    )
```
